128 devices in a mesh: dp: 128 (over x, y, z, core).
Axes of the slice: x: 4, y: 4, z: 4, core: 2. Of those that a mesh axis runs over, the one named last changes fastest.
Arguments:
- hidden_in: bfloat16 [131072, 1024], P('dp'), may hold values from -15 to 15
- lengths: int32 [128, 8], P('dp'), may hold values from 1 to 512, 1024 in all within a row
- owner: int32 [1024], P('dp'), may hold values from 0 to 1023, each once
- pooled_grad: float32 [1024, 1024], P('dp'), may hold values from -6 to 6
- norm_gain: bfloat16 [1024], replicated, may hold values from 0.25 to 1.75
- w_query: bfloat16 [1024, 2048], replicated
- w_key: bfloat16 [1024, 1024], P('dp')
- value_weight: bfloat16 [1024, 1024], P('dp'), may hold values from -0.1875 to 0.1875
- w_out: bfloat16 [2048, 1024], replicated, may hold values from -0.125 to 0.125
Outputs:
- grad_in: bfloat16 [131072, 1024], P('dp')
- grad_key: float32 [1024, 1024], P('dp')
- grad_value: float32 [1024, 1024], P('dp')
- grad_gain: float32 [1024], replicated
The draws below stay inside these ranges and needn't reach their ends.
Inputs may be any that keep to these rules, and one draw needn't show every extreme that they name: Each row of lengths sums to 1024, and some statement has exactly 512 tokens. `owner`: a permutation.
All inputs are finite; a program needn't handle non-finite values.
Results may differ from the reference program's by a relative error of at most 0.035.
The reference program's roundings to bfloat16 on the way count: a program that leaves them out, or rounds other values in their place, can miss the bound.
Values may be sent and summed in bfloat16 or wider, within the bound.
A program may use at most 128 MiB of HBM per device.

```python
import math
import jax
import jax.numpy as jnp
import numpy as np
from jax import lax

MODEL_WIDTH = 1024
QUERY_HEADS = 16
KEY_HEADS = 8
HEAD_WIDTH = 128
TOKEN_LIMIT = 1024
STATEMENT_LIMIT = 8
LMAX = 512
STMTS = 1024
QUERY_PER_KEY = 2
N_DP = 128


def draw_hidden_in(key, part):
    rows = N_DP * TOKEN_LIMIT
    block_cols = MODEL_WIDTH // N_DP
    pairing = jax.random.permutation(jax.random.fold_in(key, 13), N_DP)
    row_block = jnp.arange(rows, dtype=jnp.int32) // TOKEN_LIMIT
    col_block = jnp.arange(MODEL_WIDTH, dtype=jnp.int32) // block_cols
    spike = jnp.where(jnp.take(pairing, row_block)[:, None] == col_block[None, :], 3.0, 1.0)
    value_rows = jax.random.truncated_normal(jax.random.fold_in(key, 11), -5.0, 5.0, (rows, MODEL_WIDTH), jnp.float32)
    return (value_rows * spike).astype(jnp.bfloat16)


def key_projection_rows(key):
    sampled_values = jax.random.truncated_normal(jax.random.fold_in(key, 21), -6.0, 6.0, (MODEL_WIDTH, KEY_HEADS * HEAD_WIDTH), jnp.float32)
    return sampled_values * MODEL_WIDTH ** (-0.5)


def draw_w_key(key, part):
    return key_projection_rows(key).astype(jnp.bfloat16)


def draw_w_query(key, part):
    own = jax.random.truncated_normal(jax.random.fold_in(key, 22), -6.0, 6.0, (MODEL_WIDTH, QUERY_HEADS * HEAD_WIDTH), jnp.float32) * MODEL_WIDTH ** (-0.5)
    return own.astype(jnp.bfloat16)


def block_levels(key, shape, shards, low, high):
    def one(axis_at, shards_of):
        steps = jax.random.uniform(jax.random.fold_in(jax.random.fold_in(key, 6), axis_at), (shards_of,), jnp.float32, low / len(shards), high / len(shards))
        return jnp.repeat(jnp.exp(steps), shape[axis_at] // shards_of).reshape((-1,) + (1,) * (len(shape) - axis_at - 1))

    level = one(*shards[0])
    for cut in shards[1:]:
        level = level * one(*cut)
    return level


def length_profile(amount, total, reach, skew):
    loads = [(1 << 20) // math.isqrt(rank ** skew) + 1 for rank in range(2, amount + 1)]
    spare, counts = total - reach - (amount - 1), [1] * (amount - 1)
    while spare > 0:
        movable = [i for i in range(amount - 1) if counts[i] < reach]
        pool, remaining = sum([loads[i] for i in movable]), spare
        for i in movable:
            extra = min(reach - counts[i], max(1, remaining * loads[i] // pool), spare)
            counts[i] = counts[i] + extra
            spare = spare - extra
    return np.array([reach] + counts)


def uneven(rng, amount, total, bound, lean):
    if amount == 2:
        one = jax.random.randint(rng, (), max(1, total - bound), min(bound, total - 1) + 1)
        return jnp.stack([one, total - one])
    sizes = jnp.asarray(length_profile(amount, total, bound, lean), jnp.int32)
    twos = (amount - 1) // 2
    source_of, sink = sizes[1:1 + 2 * twos:2], sizes[2:2 + 2 * twos:2]
    slack = jnp.minimum(source_of - 1, bound - sink)
    moved = jax.random.randint(jax.random.fold_in(rng, 1), (twos,), 0, 1 << 20) % (slack + 1)
    sizes = sizes.at[1:1 + 2 * twos:2].set(source_of - moved).at[2:2 + 2 * twos:2].set(sink + moved)
    return sizes[jax.random.permutation(jax.random.fold_in(rng, 2), amount)]


def centred(own_key, shape, spread, bound, split=(), kind=jnp.bfloat16):
    result = jax.random.normal(own_key, shape, jnp.float32) * spread
    if len(split) > 0:
        result = block_levels(own_key, shape, split, -0.22, 0.18) * result
    return jnp.clip(result, min=-bound, max=bound).astype(kind)


def setup_inputs(seed: int = 0) -> dict:
    key_list = jax.random.split(jax.random.key(seed), 10)
    return {
        "hidden_in": draw_hidden_in(jax.random.fold_in(key_list[9], 71), 0),
        "lengths": jax.vmap(lambda own: uneven(own, STATEMENT_LIMIT, TOKEN_LIMIT, LMAX, 2))(jax.random.split(key_list[1], N_DP)).reshape((N_DP, STATEMENT_LIMIT)).astype(jnp.int32),
        "owner": jax.random.permutation(key_list[2], STMTS).astype(jnp.int32),
        "pooled_grad": centred(key_list[3], (STMTS, MODEL_WIDTH), 1.0, 6.0, ((0, 128),), jnp.float32),
        "norm_gain": jnp.clip(1.0 + 0.15 * jax.random.normal(key_list[4], (MODEL_WIDTH,), jnp.float32), 0.25, 1.75).astype(jnp.bfloat16),
        "w_query": draw_w_query(jax.random.fold_in(key_list[9], 71), 0),
        "w_key": draw_w_key(jax.random.fold_in(key_list[9], 71), 0),
        "value_weight": centred(key_list[7], (MODEL_WIDTH, KEY_HEADS * HEAD_WIDTH), MODEL_WIDTH ** -0.5, 0.1875, ((0, 128),)),
        "w_out": centred(key_list[8], (QUERY_HEADS * HEAD_WIDTH, MODEL_WIDTH), (QUERY_HEADS * HEAD_WIDTH) ** -0.5, 0.125),
    }


def block_pass(inputs, row_lengths, cached, norm_gain, w_query, w_key, value_weight, w_out):
    key_value_width = KEY_HEADS * HEAD_WIDTH
    scale_q = 1.0 / HEAD_WIDTH ** 0.5
    inputs_f = inputs.astype(jnp.float32)
    inv_rms = lax.rsqrt(lax.optimization_barrier(jnp.mean(inputs_f * inputs_f, axis=-1, keepdims=True)) + 1e-06)
    normed = inputs_f * inv_rms
    normed_b = (normed * norm_gain.astype(jnp.float32)).astype(jnp.bfloat16)
    key_rows = jnp.dot(normed_b, w_key, preferred_element_type=jnp.float32).astype(jnp.bfloat16)
    value_rows = jnp.dot(normed_b, value_weight, preferred_element_type=jnp.float32).astype(jnp.bfloat16)
    ends = jnp.cumsum(row_lengths).astype(jnp.int32)
    last_rows = (ends - 1).astype(jnp.int32)
    positions = jnp.arange(TOKEN_LIMIT, dtype=jnp.int32)
    segment = lax.optimization_barrier(jnp.sum((positions[:, None] >= ends[None, :]).astype(jnp.int32), axis=1))
    member = segment[None, :] == jnp.arange(STATEMENT_LIMIT, dtype=jnp.int32)[:, None]
    last_normed = jnp.take(normed_b, last_rows, axis=0)
    query_rows = jnp.dot(last_normed, w_query, preferred_element_type=jnp.float32).astype(jnp.bfloat16)
    query_rows = query_rows.reshape(STATEMENT_LIMIT, KEY_HEADS, QUERY_PER_KEY, HEAD_WIDTH).astype(jnp.float32)
    key_rows_float = key_rows.reshape(TOKEN_LIMIT, KEY_HEADS, HEAD_WIDTH).astype(jnp.float32)
    value_rows_float = value_rows.reshape(TOKEN_LIMIT, KEY_HEADS, HEAD_WIDTH).astype(jnp.float32)
    scores = jnp.einsum('sgqe,tge->sgqt', query_rows, key_rows_float) * scale_q
    scores = jnp.where(member[:, None, None, :], scores, -1e+30)
    top = lax.optimization_barrier(jnp.max(scores, axis=-1, keepdims=True))
    expo = jnp.exp(scores - top)
    probs = expo / lax.optimization_barrier(jnp.sum(expo, axis=-1, keepdims=True))
    probs_b = probs.astype(jnp.bfloat16).astype(jnp.float32)
    attended = jnp.einsum('sgqt,tge->sgqe', probs_b, value_rows_float).astype(jnp.bfloat16)
    attended = attended.reshape(STATEMENT_LIMIT, QUERY_HEADS * HEAD_WIDTH)
    pooled = jnp.take(inputs_f, last_rows, axis=0) + jnp.dot(attended, w_out, preferred_element_type=jnp.float32)
    inv_len = lax.rsqrt(lax.optimization_barrier(jnp.sum(pooled * pooled, axis=-1, keepdims=True)) + 1e-06)
    embed = pooled * inv_len
    grad_pool = inv_len * (cached - embed * lax.optimization_barrier(jnp.sum(embed * cached, axis=-1, keepdims=True)))
    grad_pool_b = grad_pool.astype(jnp.bfloat16)
    attention_gradient = jnp.dot(grad_pool_b, w_out.T, preferred_element_type=jnp.float32).astype(jnp.bfloat16)
    attention_gradient = attention_gradient.reshape(STATEMENT_LIMIT, KEY_HEADS, QUERY_PER_KEY, HEAD_WIDTH).astype(jnp.float32)
    grad_prob = jnp.einsum('sgqe,tge->sgqt', attention_gradient, value_rows_float)
    grad_score = probs * (grad_prob - lax.optimization_barrier(jnp.sum(probs * grad_prob, axis=-1, keepdims=True))) * scale_q
    grad_score = grad_score.astype(jnp.bfloat16).astype(jnp.float32)
    grad_query = jnp.einsum('sgqt,tge->sgqe', grad_score, key_rows_float).astype(jnp.bfloat16).reshape(STATEMENT_LIMIT, QUERY_HEADS * HEAD_WIDTH)
    grad_keys = jnp.einsum('sgqt,sgqe->tge', grad_score, query_rows).astype(jnp.bfloat16).reshape(TOKEN_LIMIT, key_value_width)
    grad_values = jnp.einsum('sgqt,sgqe->tge', probs_b, attention_gradient).astype(jnp.bfloat16).reshape(TOKEN_LIMIT, key_value_width)
    grad_normed = jnp.dot(grad_keys, w_key.T, preferred_element_type=jnp.float32)
    grad_normed = grad_normed + jnp.dot(grad_values, value_weight.T, preferred_element_type=jnp.float32)
    grad_normed = grad_normed.at[last_rows].add(jnp.dot(grad_query, w_query.T, preferred_element_type=jnp.float32))
    gain_part = lax.optimization_barrier(jnp.sum(grad_normed * normed, axis=0))
    scaled = grad_normed * norm_gain.astype(jnp.float32)
    grad_in = inv_rms * (scaled - normed * lax.optimization_barrier(jnp.mean(scaled * normed, axis=-1, keepdims=True)))
    grad_in = grad_in.at[last_rows].add(grad_pool).astype(jnp.bfloat16)
    both = jnp.concatenate([grad_keys, grad_values], axis=1)
    weight_part = lax.dot_general(normed_b, both, (((0,), (0,)), ((), ())), preferred_element_type=jnp.float32)
    return (grad_in, weight_part, gain_part)

def reference(hidden_in, lengths, owner, pooled_grad, norm_gain, w_query, w_key, value_weight, w_out):
    key_value_width = KEY_HEADS * HEAD_WIDTH
    cached_all = jnp.take(pooled_grad, owner.astype(jnp.int32), axis=0).reshape(N_DP, STATEMENT_LIMIT, MODEL_WIDTH)
    blocks = hidden_in.reshape(N_DP, TOKEN_LIMIT, MODEL_WIDTH)

    def step_fn(carry, items):
        block, row_lengths, cached = items
        grad_in, weight_part, gain_part = block_pass(block, row_lengths, cached, norm_gain, w_query, w_key, value_weight, w_out)
        return ((carry[0] + weight_part, carry[1] + gain_part), grad_in)
    init = (jnp.zeros((MODEL_WIDTH, 2 * key_value_width), jnp.float32), jnp.zeros((MODEL_WIDTH,), jnp.float32))
    totals, grads = lax.scan(step_fn, init, (blocks, lengths, cached_all))
    weight_total, gain_total = totals
    return (grads.reshape(N_DP * TOKEN_LIMIT, MODEL_WIDTH), weight_total[:, :key_value_width], weight_total[:, key_value_width:], gain_total)
```

```python
import functools
import jax
import jax.numpy as jnp
from jax import lax
from jax.experimental import pallas as pl
from jax.experimental.pallas import tpu as pltpu
from jax.sharding import PartitionSpec as P

QUERY_HEADS = 16
KEY_HEADS = 8
HEAD_WIDTH = 128
RING = 4
STRIDES = (32, 8, 2)
ORDERS = ((0, 1, 2), (1, 2, 0), (2, 0, 1))
MESH = pl.DeviceIdType.MESH


def place():
    me = lax.axis_index("dp")
    return me, ((me // 32) % 4, (me // 8) % 4, (me // 2) % 4), me % 2


def peer_of(me, coords, dim, delta):
    there = (coords[dim] + delta) % RING
    return there, me + (there - coords[dim]) * STRIDES[dim]


def greet(me, coords, core):
    barrier = pltpu.get_barrier_semaphore()
    pl.semaphore_signal(barrier, inc=1, device_id=(me + 1 - 2 * core,), device_id_type=MESH)
    for dim in range(3):
        for delta in range(1, RING):
            _, other = peer_of(me, coords, dim, delta)
            pl.semaphore_signal(barrier, inc=1, device_id=(other,), device_id_type=MESH)
    pl.semaphore_wait(barrier, 10)


def send(src, dst, sems, where, other):
    copy = pltpu.make_async_remote_copy(
        src_ref=src,
        dst_ref=dst,
        send_sem=sems.at[(0,) + where],
        recv_sem=sems.at[(1,) + where],
        device_id=(other,),
        device_id_type=MESH,
    )
    copy.start()
    return copy


def slab(ref, coords, core, dims):
    index = [coords[0], coords[1], coords[2], core]
    for dim in dims:
        index[dim] = slice(None)
    return ref.at[tuple(index)]


def gather_kernel(key_ref, value_ref, grad_ref, kv_out, grad_out, sems, pair_sems, own_sems):
    me, coords, core = place()
    sibling = me + 1 - 2 * core
    width = key_ref.shape[1]
    sources = (key_ref, value_ref, grad_ref)
    targets = (
        kv_out.at[:, :, :, :, :, pl.ds(0, width)],
        kv_out.at[:, :, :, :, :, pl.ds(width, width)],
        grad_out,
    )
    own = []
    for part in range(3):
        copy = pltpu.make_async_copy(
            sources[part], slab(targets[part], coords, core, ()), own_sems.at[part]
        )
        copy.start()
        own.append(copy)
    greet(me, coords, core)
    stages = [[], [], []]
    for part in range(3):
        dim = ORDERS[part][0]
        for delta in range(1, RING):
            _, other = peer_of(me, coords, dim, delta)
            stages[part].append(
                send(
                    sources[part],
                    slab(targets[part], coords, core, ()),
                    sems,
                    (part, 0, delta - 1),
                    other,
                )
            )
    last = [[], [], []]
    for step in (1, 2):
        for part in range(3):
            if step == 1:
                own[part].wait()
            for copy in stages[part]:
                copy.wait()
            stages[part] = []
            done = ORDERS[part][:step]
            dim = ORDERS[part][step]
            piece = slab(targets[part], coords, core, done)
            for delta in (2, 1, 3):
                _, other = peer_of(me, coords, dim, delta)
                stages[part].append(send(piece, piece, sems, (part, step, delta - 1), other))
            if step == 2:
                last[part].append(send(piece, piece, pair_sems, (part, 0), sibling))
    for part in range(3):
        dim = ORDERS[part][2]
        done = ORDERS[part][:2]
        for at, delta in ((1, 1), (2, 3), (0, 2)):
            stages[part][at].wait()
            there = list(coords)
            there[dim] = (coords[dim] + RING - delta) % RING
            piece = slab(targets[part], there, core, done)
            last[part].append(send(piece, piece, pair_sems, (part, delta), sibling))
    for part in range(3):
        for copy in last[part]:
            copy.wait()


def gather_all(key_rows, value_rows, grad_rows):
    rows, width = key_rows.shape
    grid = (RING, RING, RING, 2, rows)
    kv, grads = pl.pallas_call(
        gather_kernel,
        out_shape=(
            jax.ShapeDtypeStruct(grid + (2 * width,), jnp.bfloat16),
            jax.ShapeDtypeStruct(grid + (width,), jnp.bfloat16),
        ),
        in_specs=[pl.BlockSpec(memory_space=pltpu.VMEM)] * 3,
        out_specs=(
            pl.BlockSpec(memory_space=pltpu.VMEM),
            pl.BlockSpec(memory_space=pltpu.VMEM),
        ),
        scratch_shapes=[
            pltpu.SemaphoreType.DMA((2, 3, 3, 3)),
            pltpu.SemaphoreType.DMA((2, 3, 4)),
            pltpu.SemaphoreType.DMA((3,)),
        ],
        compiler_params=pltpu.CompilerParams(
            collective_id=0, has_side_effects=True, vmem_limit_bytes=40 * 2**20
        ),
        name="gather_rows",
    )(key_rows, value_rows, grad_rows)
    total = 2 * RING**3 * rows
    return kv.reshape(total, 2 * width), grads.reshape(total, width)


def f32(value):
    return value.astype(jnp.float32)


def scatter_kernel(cuts, share_ref, gain_ref, out_ref, gain_out, *scratch):
    pair_in, first, first_in, second, second_in, third, third_in = (
        scratch[3 * i : 3 * i + 3] for i in range(7)
    )
    gain_pair, gain_sum, gain_in, sems, pair_sems, gain_sems, gain_pair_sem = scratch[21:]
    me, coords, core = place()
    sibling = me + 1 - 2 * core
    greet(me, coords, core)
    gain_copy = send(gain_ref, gain_pair, gain_pair_sem, (0,), sibling)
    pairs = []
    for part, (low, size) in enumerate(cuts):
        pairs.append(
            send(
                share_ref.at[:, :, :, 1 - core, :, pl.ds(low, size)],
                pair_in[part],
                pair_sems,
                (part,),
                sibling,
            )
        )

    def gain_round(dim, value):
        gain_sum[dim] = value
        gain_in[dim, coords[dim]] = value
        copies = []
        for delta in range(1, RING):
            _, other = peer_of(me, coords, dim, delta)
            copies.append(
                send(
                    gain_sum.at[dim],
                    gain_in.at[dim, coords[dim]],
                    gain_sems,
                    (dim, delta - 1),
                    other,
                )
            )
        return copies

    def gain_total(dim, copies):
        for copy in copies:
            copy.wait()
        return (gain_in[dim, 0] + gain_in[dim, 1]) + (gain_in[dim, 2] + gain_in[dim, 3])

    def push(part, step, source, target):
        copies = []
        for delta in (2, 1, 3):
            there, other = peer_of(me, coords, ORDERS[part][step], delta)
            copies.append(
                send(source.at[there], target.at[delta - 1], sems, (part, step, delta - 1), other)
            )
        return copies

    gain_copy.wait()
    gain_copies = gain_round(0, gain_ref[...] + gain_pair[...])
    flights = []
    for part, (low, size) in enumerate(cuts):
        pairs[part].wait()
        order = ORDERS[part]

        @pl.loop(0, RING * RING)
        def _(at):
            ahead = [at // RING, at % RING, 0]
            for z in range(RING):
                ahead[2] = z
                value = f32(share_ref[ahead[0], ahead[1], z, core, :, pl.ds(low, size)])
                value = value + f32(pair_in[part][ahead[0], ahead[1], z])
                first[part][ahead[order[0]], ahead[order[1]], ahead[order[2]]] = value.astype(
                    jnp.bfloat16
                )

        flights.append(push(part, 0, first[part], first_in[part]))
    gain_copies = gain_round(1, gain_total(0, gain_copies))
    for part in range(3):
        for copy in flights[part]:
            copy.wait()
        mine = coords[ORDERS[part][0]]

        @pl.loop(0, RING)
        def _(a):
            for b in range(RING):
                value = f32(first[part][mine, a, b]) + f32(first_in[part][0, a, b])
                value = value + (f32(first_in[part][1, a, b]) + f32(first_in[part][2, a, b]))
                second[part][a, b] = value.astype(jnp.bfloat16)

        flights[part] = push(part, 1, second[part], second_in[part])
    gain_copies = gain_round(2, gain_total(1, gain_copies))
    for part in range(3):
        for copy in flights[part]:
            copy.wait()
        mine = coords[ORDERS[part][1]]
        for b in range(RING):
            value = f32(second[part][mine, b]) + f32(second_in[part][0, b])
            value = value + (f32(second_in[part][1, b]) + f32(second_in[part][2, b]))
            third[part][b] = value.astype(jnp.bfloat16)
        flights[part] = push(part, 2, third[part], third_in[part])
    gain_out[...] = gain_total(2, gain_copies)
    for part, (low, size) in enumerate(cuts):
        for copy in flights[part]:
            copy.wait()
        mine = coords[ORDERS[part][2]]
        value = f32(third[part][mine]) + f32(third_in[part][0])
        value = value + (f32(third_in[part][1]) + f32(third_in[part][2]))
        out_ref[:, pl.ds(low, size)] = value


def scatter_sum(share, gain):
    total, width = share.shape
    rows = total // (2 * RING**3)
    lanes = width // 128
    sizes = [128 * ((lanes + 2 - part) // 3) for part in range(3)]
    cuts, low = [], 0
    for size in sizes:
        cuts.append((low, size))
        low += size

    def scratch(*lead):
        return [pltpu.VMEM(lead + (rows, size), jnp.bfloat16) for _, size in cuts]

    out, gain_total = pl.pallas_call(
        functools.partial(scatter_kernel, tuple(cuts)),
        out_shape=(
            jax.ShapeDtypeStruct((rows, width), jnp.float32),
            jax.ShapeDtypeStruct((8, gain.shape[0] // 8), jnp.float32),
        ),
        in_specs=[pl.BlockSpec(memory_space=pltpu.VMEM)] * 2,
        out_specs=(
            pl.BlockSpec(memory_space=pltpu.VMEM),
            pl.BlockSpec(memory_space=pltpu.VMEM),
        ),
        scratch_shapes=scratch(RING, RING, RING)
        + scratch(RING, RING, RING)
        + scratch(RING - 1, RING, RING)
        + scratch(RING, RING)
        + scratch(RING - 1, RING)
        + scratch(RING)
        + scratch(RING - 1)
        + [
            pltpu.VMEM((8, gain.shape[0] // 8), jnp.float32),
            pltpu.VMEM((3, 8, gain.shape[0] // 8), jnp.float32),
            pltpu.VMEM((3, RING, 8, gain.shape[0] // 8), jnp.float32),
            pltpu.SemaphoreType.DMA((2, 3, 3, 3)),
            pltpu.SemaphoreType.DMA((2, 3)),
            pltpu.SemaphoreType.DMA((2, 3, 3)),
            pltpu.SemaphoreType.DMA((2, 1)),
        ],
        compiler_params=pltpu.CompilerParams(
            collective_id=1, has_side_effects=True, vmem_limit_bytes=40 * 2**20
        ),
        name="scatter_sum",
    )(share.reshape(RING, RING, RING, 2, rows, width), gain.reshape(8, -1))
    return out, gain_total.reshape(-1)


def per_device(
    hidden_in, lengths, owner, pooled_grad, norm_gain, w_query, w_key, value_weight, w_out
):
    token_rows = hidden_in.shape[0]
    statement_slots = lengths.shape[1]
    key_value_width = w_key.shape[1]
    head_groups = QUERY_HEADS // KEY_HEADS
    scale_q = 1.0 / HEAD_WIDTH**0.5
    kv_full, every_grad = gather_all(w_key, value_weight, pooled_grad.astype(jnp.bfloat16))
    cached = jnp.take(every_grad, owner, axis=0).astype(jnp.float32)
    inputs_f = hidden_in.astype(jnp.float32)
    inv_rms = lax.rsqrt(jnp.mean(inputs_f * inputs_f, axis=-1, keepdims=True) + 1e-06)
    normed = inputs_f * inv_rms
    normed_b = (normed * norm_gain.astype(jnp.float32)).astype(jnp.bfloat16)
    key_value_joint = jnp.dot(normed_b, kv_full, preferred_element_type=jnp.float32)
    key_value_joint = key_value_joint.astype(jnp.bfloat16)
    key_rows = key_value_joint[:, :key_value_width].reshape(token_rows, KEY_HEADS, HEAD_WIDTH)
    value_rows = key_value_joint[:, key_value_width:].reshape(token_rows, KEY_HEADS, HEAD_WIDTH)
    ends = jnp.cumsum(lengths[0])
    last_rows = ends - 1
    positions = jnp.arange(token_rows, dtype=jnp.int32)
    segment = jnp.sum((positions[:, None] >= ends[None, :]).astype(jnp.int32), axis=1)
    member = segment[None, :] == jnp.arange(statement_slots, dtype=jnp.int32)[:, None]
    last_normed = jnp.take(normed_b, last_rows, axis=0)
    query_rows = jnp.dot(last_normed, w_query, preferred_element_type=jnp.float32).astype(
        jnp.bfloat16
    )
    query_rows = query_rows.reshape(statement_slots, KEY_HEADS, head_groups, HEAD_WIDTH)
    scores = (
        jnp.einsum("sgqe,tge->sgqt", query_rows, key_rows, preferred_element_type=jnp.float32)
        * scale_q
    )
    scores = jnp.where(member[:, None, None, :], scores, -1e30)
    top = jnp.max(scores, axis=-1, keepdims=True)
    expo = jnp.exp(scores - top)
    probs = expo / jnp.sum(expo, axis=-1, keepdims=True)
    probs_b = probs.astype(jnp.bfloat16)
    attended = jnp.einsum(
        "sgqt,tge->sgqe", probs_b, value_rows, preferred_element_type=jnp.float32
    ).astype(jnp.bfloat16)
    attended = attended.reshape(statement_slots, QUERY_HEADS * HEAD_WIDTH)
    pooled = jnp.take(inputs_f, last_rows, axis=0) + jnp.dot(
        attended, w_out, preferred_element_type=jnp.float32
    )
    inv_len = lax.rsqrt(jnp.sum(pooled * pooled, axis=-1, keepdims=True) + 1e-06)
    embed = pooled * inv_len
    grad_pool = inv_len * (cached - embed * jnp.sum(embed * cached, axis=-1, keepdims=True))
    grad_pool_b = grad_pool.astype(jnp.bfloat16)
    attention_gradient = lax.dot_general(
        grad_pool_b, w_out, (((1,), (1,)), ((), ())), preferred_element_type=jnp.float32
    )
    attention_gradient = attention_gradient.astype(jnp.bfloat16).reshape(
        statement_slots, KEY_HEADS, head_groups, HEAD_WIDTH
    )
    grad_values = jnp.einsum(
        "sgqt,sgqe->tge", probs_b, attention_gradient, preferred_element_type=jnp.float32
    )
    grad_values = grad_values.astype(jnp.bfloat16).reshape(token_rows, key_value_width)
    grad_prob = jnp.einsum(
        "sgqe,tge->sgqt", attention_gradient, value_rows, preferred_element_type=jnp.float32
    )
    grad_score = probs * (grad_prob - jnp.sum(probs * grad_prob, axis=-1, keepdims=True)) * scale_q
    grad_score = grad_score.astype(jnp.bfloat16)
    grad_query = jnp.einsum(
        "sgqt,tge->sgqe", grad_score, key_rows, preferred_element_type=jnp.float32
    )
    grad_query = grad_query.astype(jnp.bfloat16).reshape(statement_slots, QUERY_HEADS * HEAD_WIDTH)
    grad_keys = jnp.einsum(
        "sgqt,sgqe->tge", grad_score, query_rows, preferred_element_type=jnp.float32
    )
    grad_keys = grad_keys.astype(jnp.bfloat16).reshape(token_rows, key_value_width)
    grad_both = jnp.concatenate([grad_keys, grad_values], axis=1)
    grad_normed = lax.dot_general(
        grad_both, kv_full, (((1,), (1,)), ((), ())), preferred_element_type=jnp.float32
    )
    query_back = lax.dot_general(
        grad_query, w_query, (((1,), (1,)), ((), ())), preferred_element_type=jnp.float32
    )
    grad_normed = grad_normed.at[last_rows].add(query_back)
    gain_part = jnp.sum(grad_normed * normed, axis=0)
    scaled = grad_normed * norm_gain.astype(jnp.float32)
    grad_in = inv_rms * (scaled - normed * jnp.mean(scaled * normed, axis=-1, keepdims=True))
    grad_in = grad_in.at[last_rows].add(grad_pool).astype(jnp.bfloat16)
    share = lax.dot_general(
        normed_b, grad_both, (((0,), (0,)), ((), ())), preferred_element_type=jnp.float32
    ).astype(jnp.bfloat16)
    weight_share, gain_total = scatter_sum(share, gain_part)
    return (
        grad_in,
        weight_share[:, :key_value_width],
        weight_share[:, key_value_width:],
        gain_total,
    )


def solution(mesh):
    return jax.shard_map(
        per_device,
        mesh=mesh,
        in_specs=(
            P("dp", None),
            P("dp", None),
            P("dp"),
            P("dp", None),
            P(),
            P(),
            P("dp", None),
            P("dp", None),
            P(),
        ),
        out_specs=(P("dp", None), P("dp", None), P("dp", None), P()),
        check_vma=False,
    )
```

```python
import functools
import jax
import jax.numpy as jnp
from jax import lax
from jax.experimental import pallas as pl
from jax.experimental.pallas import tpu as pltpu
from jax.sharding import PartitionSpec as P

QUERY_HEADS = 16
KEY_HEADS = 8
HEAD_WIDTH = 128
WIDTH = KEY_HEADS * HEAD_WIDTH
SLOTS = 8
TILE = 256
RING = 4
STRIDES = (32, 8, 2)
ORDERS = ((0, 1, 2), (1, 2, 0), (2, 0, 1))
MESH = pl.DeviceIdType.MESH
BF16, F32 = jnp.bfloat16, jnp.float32
GATHER_CUTS = (
    ((0, 384), (384, 384), (768, 256)),
    ((0, 256), (256, 384), (640, 384)),
    ((0, 384), (384, 256), (640, 384)),
)
SCATTER_CUTS = ((0, 768), (768, 640), (1408, 640))


def f32(value):
    return value.astype(F32)


def dot(a, b, ca=1, cb=0):
    return lax.dot_general(a, b, (((ca,), (cb,)), ((), ())), preferred_element_type=F32)


class Net:
    def __init__(self, sems):
        self.sems, self.used = sems, 0
        me = lax.axis_index("dp")
        self.me = me
        self.coords = ((me // 32) % RING, (me // 8) % RING, (me // 2) % RING)
        self.core = me % 2
        self.sibling = me + 1 - 2 * self.core

    def at(self, dim, delta):
        return (self.coords[dim] + delta + RING) % RING

    def peer(self, dim, delta):
        return self.me + (self.at(dim, delta) - self.coords[dim]) * STRIDES[dim]

    def greet(self):
        barrier = pltpu.get_barrier_semaphore()
        pl.semaphore_signal(barrier, inc=1, device_id=(self.sibling,), device_id_type=MESH)
        for dim in range(3):
            for delta in range(1, RING):
                pl.semaphore_signal(
                    barrier, inc=1, device_id=(self.peer(dim, delta),), device_id_type=MESH
                )
        pl.semaphore_wait(barrier, 10)

    def send(self, src, dst, other):
        copy = pltpu.make_async_remote_copy(
            src_ref=src,
            dst_ref=dst,
            send_sem=self.sems.at[0, self.used],
            recv_sem=self.sems.at[1, self.used],
            device_id=(other,),
            device_id_type=MESH,
        )
        self.used += 1
        copy.start()
        return copy

    def local(self, src, dst):
        copy = pltpu.make_async_copy(src, dst, self.sems.at[0, self.used])
        self.used += 1
        copy.start()
        return copy


def finish(copies):
    for copy in copies:
        copy.wait()
    copies.clear()


class Gather:
    def __init__(self, net, source, target, low, size, order):
        self.net, self.order = net, order
        self.source = source.at[:, pl.ds(low, size)]
        self.target = target.at[:, :, :, :, :, pl.ds(low, size)]
        self.flying, self.paired = [], []

    def slab(self, done, dim=None, delta=0, half=None):
        net = self.net
        index = [net.coords[0], net.coords[1], net.coords[2], net.core]
        if dim is not None:
            index[dim] = net.at(dim, delta)
        for at in done:
            index[at] = slice(None)
        if half is not None:
            index[done[0]] = pl.ds(half * 2, 2)
        return self.target.at[tuple(index)]

    def open(self):
        net, mine = self.net, self.slab(())
        self.own = net.local(self.source, mine)
        for delta in (2, 1, 3):
            self.flying.append(net.send(self.source, mine, net.peer(self.order[0], delta)))

    def pair(self, step, delta):
        piece = self.slab(self.order[:step], self.order[step], delta)
        self.paired.append(self.net.send(piece, piece, self.net.sibling))

    def ring(self, step):
        if step == 1:
            self.own.wait()
        finish(self.flying)
        dim, piece = self.order[step], self.slab(self.order[:step])
        for delta in (1, 3):
            self.flying.append(self.net.send(piece, piece, self.net.peer(dim, delta)))
        if step == 2:
            self.pair(2, 0)

    def relay(self, step):
        finish(self.flying)
        dim, done = self.order[step], self.order[:step]
        for half, delta in ((0, 1), (1, 3)):
            piece = self.slab(done, dim, RING - delta, half)
            self.flying.append(self.net.send(piece, piece, self.net.peer(dim, delta)))
        if step == 2:
            self.pair(2, 1)
            self.pair(2, 3)

    def close(self):
        finish(self.flying)
        self.pair(2, 2)


def step_kernel(
    lengths,
    owner,
    hidden_hbm,
    grad_ref,
    gain_ref,
    query_hbm,
    key_ref,
    value_ref,
    out_hbm,
    grad_in,
    weight_grad,
    gain_grad,
    *scratch,
):
    (hid, wq, wo, kv, every, grad_b, nb, nbt, inv_s, joint, both, result) = scratch[:12]
    (score, prob, gscore, q_all, a_all, flat, flat_b, select_rows, pool_rows) = scratch[12:21]
    (share, gain_acc, gain_pair, gain_sum, gain_in, sems) = scratch[21:27]
    pair_in, first, relay_in, first_in, second, second_in, third, third_in = (
        scratch[27 + 3 * i : 30 + 3 * i] for i in range(8)
    )
    net = Net(sems)
    scale_q = 1.0 / HEAD_WIDTH**0.5
    tokens = nb.shape[0]
    tiles = tokens // TILE
    blocks = TILE // SLOTS

    hid_copy = net.local(hidden_hbm, hid)
    wq_copy = net.local(query_hbm, wq)
    grad_b[...] = grad_ref[...].astype(BF16)
    net.greet()
    key_parts, value_parts, grad_parts = (
        [
            Gather(net, source, target, low, size, ORDERS[part])
            for part, (low, size) in enumerate(cuts)
        ]
        for source, target, cuts in (
            (key_ref, kv.at[:, :, :, :, :, pl.ds(0, WIDTH)], GATHER_CUTS[0]),
            (value_ref, kv.at[:, :, :, :, :, pl.ds(WIDTH, WIDTH)], GATHER_CUTS[1]),
            (grad_b, every, GATHER_CUTS[2]),
        )
    )
    for part in key_parts + value_parts + grad_parts:
        part.open()
    wo_copy = net.local(out_hbm, wo)
    gain = f32(gain_ref[...])

    def norm_tile(i):
        rows = pl.ds(pl.multiple_of(i * TILE, TILE), TILE)
        x = f32(hid[pl.ds(i * blocks, blocks)]).reshape(TILE, WIDTH)
        inv = lax.rsqrt(jnp.mean(x * x, axis=-1, keepdims=True) + 1e-06)
        inv_s[rows, :] = inv
        y = (x * inv) * gain
        nb[rows, :] = y.astype(BF16)
        nbt[:, rows] = y.T.astype(BF16)

    hid_copy.wait()

    @pl.loop(0, tiles // 2)
    def _(i):
        norm_tile(i)

    for part in key_parts:
        part.ring(1)
    for part in value_parts:
        part.ring(1)

    @pl.loop(tiles // 2, tiles)
    def _(i):
        norm_tile(i)

    for part in key_parts:
        part.relay(1)
    for part in value_parts:
        part.relay(1)

    row8 = lax.broadcasted_iota(jnp.int32, (SLOTS, WIDTH), 0)
    lane = lax.broadcasted_iota(jnp.int32, (SLOTS, WIDTH), 1)
    starts = jnp.zeros((SLOTS, WIDTH), jnp.int32)
    ends = jnp.zeros((SLOTS, WIDTH), jnp.int32)
    lane_last = jnp.full((SLOTS, HEAD_WIDTH), -1, jnp.int32)
    short_lane = lax.broadcasted_iota(jnp.int32, (SLOTS, HEAD_WIDTH), 1)
    hidden_last = jnp.zeros((SLOTS, WIDTH), F32)
    at = jnp.int32(0)
    for s in range(SLOTS):
        starts = jnp.where(row8 == s, at, starts)
        at = at + lengths[0, s]
        ends = jnp.where(row8 == s, at, ends)
        last = jnp.maximum(at - 1, 0)
        chosen = (short_lane % SLOTS == s) & (short_lane < 3 * SLOTS)
        lane_last = jnp.where(chosen, last, lane_last)
        block = f32(hid[last // SLOTS])
        picked = jnp.sum(jnp.where(row8 == last % SLOTS, block, 0.0), axis=0, keepdims=True)
        hidden_last = jnp.where(row8 == s, picked, hidden_last)
    member = (lane >= starts) & (lane < ends)
    inv_last = lax.rsqrt(jnp.mean(hidden_last * hidden_last, axis=-1, keepdims=True) + 1e-06)
    normed_last = hidden_last * inv_last
    last_b = (normed_last * gain).astype(BF16)

    for part in key_parts:
        part.ring(2)
    wq_copy.wait()

    def spread(value, at, target):
        for part in range(value.shape[1] // HEAD_WIDTH):
            target[pl.ds(SLOTS * (at + part), SLOTS), :] = f32(
                value[:, part * HEAD_WIDTH : (part + 1) * HEAD_WIDTH].astype(BF16)
            )

    for n in range(4):
        spread(dot(last_b, wq[:, pl.ds(512 * n, 512)]), 4 * n, q_all)
    for part in value_parts:
        part.ring(2)
    for part in key_parts:
        part.relay(2)
    for part in grad_parts:
        part.ring(1)
    for part in value_parts:
        part.relay(2)
    for part in key_parts:
        part.close()
    for part in grad_parts:
        part.relay(1)
    for part in key_parts:
        finish(part.paired)

    def project(i, low):
        rows = pl.ds(pl.multiple_of(i * TILE, TILE), TILE)
        weight = kv[:, :, :, :, :, pl.ds(low, WIDTH)].reshape(WIDTH, WIDTH)
        joint[rows, pl.ds(low, WIDTH)] = dot(nb[rows, :], weight).astype(BF16)

    @pl.loop(0, tiles // 2)
    def _(i):
        project(i, 0)

    for part in value_parts:
        part.close()
    for part in grad_parts:
        part.ring(2)

    @pl.loop(tiles // 2, tiles)
    def _(i):
        project(i, 0)

    for part in value_parts:
        finish(part.paired)
    for part in grad_parts:
        part.relay(2)

    @pl.loop(0, tiles)
    def _(i):
        project(i, WIDTH)

    for part in grad_parts:
        part.close()

    def head(g, base=0):
        return pl.ds(base + g * HEAD_WIDTH, HEAD_WIDTH)

    def pair_rows(g):
        return pl.ds(2 * SLOTS * g, 2 * SLOTS)

    for g in range(KEY_HEADS):
        score[pair_rows(g), :] = dot(q_all[pair_rows(g), :].astype(BF16), joint[:, head(g)], 1, 1)
    scores = score[...].reshape(QUERY_HEADS, SLOTS, tokens) * scale_q
    scores = jnp.where(member[None], scores, -1e30)
    expo = jnp.exp(scores - jnp.max(scores, axis=-1, keepdims=True))
    probs = expo / jnp.sum(expo, axis=-1, keepdims=True)
    prob[...] = probs.reshape(QUERY_HEADS * SLOTS, tokens)

    def flatten(g, value):
        for q in range(2):
            flat[:, head(2 * g + q)] = value[q * SLOTS : (q + 1) * SLOTS, :]

    for g in range(KEY_HEADS):
        flatten(g, dot(prob[pair_rows(g), :].astype(BF16), joint[:, head(g, WIDTH)]))
    wo_copy.wait()
    pooled = hidden_last + dot(flat[...].astype(BF16), wo[...])
    for part in grad_parts:
        finish(part.paired)
    cached = jnp.zeros((SLOTS, WIDTH), F32)
    for s in range(SLOTS):
        o = owner[s]
        block = f32(every[o // 256, (o // 64) % RING, (o // 16) % RING, (o // 8) % 2])
        picked = jnp.sum(jnp.where(row8 == o % SLOTS, block, 0.0), axis=0, keepdims=True)
        cached = jnp.where(row8 == s, picked, cached)
    inv_len = lax.rsqrt(jnp.sum(pooled * pooled, axis=-1, keepdims=True) + 1e-06)
    embed = pooled * inv_len
    grad_pool = inv_len * (cached - embed * jnp.sum(embed * cached, axis=-1, keepdims=True))
    grad_pool_b = grad_pool.astype(BF16)
    for n in range(4):
        spread(dot(grad_pool_b, wo[pl.ds(512 * n, 512), :], 1, 1), 4 * n, a_all)

    def three(value):
        hi = f32(value.astype(BF16))
        mid = f32((value - hi).astype(BF16))
        rest = jnp.zeros((HEAD_WIDTH - 3 * SLOTS, WIDTH), F32)
        return jnp.concatenate([hi, mid, (value - hi) - mid, rest], axis=0).astype(BF16)

    pool_rows[...] = three(grad_pool)

    for g in range(KEY_HEADS):
        score[pair_rows(g), :] = dot(
            a_all[pair_rows(g), :].astype(BF16), joint[:, head(g, WIDTH)], 1, 1
        )
        both[:, head(g, WIDTH)] = dot(
            prob[pair_rows(g), :].astype(BF16), a_all[pair_rows(g), :].astype(BF16), 0, 0
        ).astype(BF16)
    grad_prob = score[...]
    probs = prob[...]
    inner = jnp.sum(probs * grad_prob, axis=-1, keepdims=True)
    gscore[...] = (probs * (grad_prob - inner) * scale_q).astype(BF16)
    for g in range(KEY_HEADS):
        both[:, head(g)] = dot(
            gscore[pair_rows(g), :], q_all[pair_rows(g), :].astype(BF16), 0, 0
        ).astype(BF16)

    def share_part(part):
        low, size = SCATTER_CUTS[part]

        @pl.loop(0, RING)
        def _(x):
            rows = pl.ds(pl.multiple_of(x * TILE, TILE), TILE)
            value = dot(nbt[rows, :], both[:, pl.ds(low, size)])
            share[x, :, :, :, :, pl.ds(low, size)] = value.reshape(
                RING, RING, 2, SLOTS, size
            ).astype(BF16)
            weight = f32(kv[x, :, :, :, :, pl.ds(low, size)]).reshape(TILE, size)
            product = value * weight
            total = product[:, :HEAD_WIDTH]
            for n in range(1, size // HEAD_WIDTH):
                total = total + product[:, n * HEAD_WIDTH : (n + 1) * HEAD_WIDTH]
            if part == 0:
                gain_acc[rows, :] = total
            else:
                gain_acc[rows, :] += total

        return net.send(
            share.at[:, :, :, 1 - net.core, :, pl.ds(low, size)], pair_in[part], net.sibling
        )

    flights = [[], [], []]
    early = [[], [], []]

    def halves(part):
        pairs[part].wait()
        low, size = SCATTER_CUTS[part]
        order = ORDERS[part]

        @pl.loop(0, RING * RING)
        def _(at):
            ahead = [at // RING, at % RING, 0]
            for z in range(RING):
                ahead[2] = z
                value = f32(share[ahead[0], ahead[1], z, net.core, :, pl.ds(low, size)])
                value = value + f32(pair_in[part][ahead[0], ahead[1], z])
                first[part][ahead[order[0]], ahead[order[1]], ahead[order[2]]] = value.astype(BF16)

        dim = order[0]
        for half, delta in ((0, 1), (1, 3)):
            flights[part].append(
                net.send(
                    first[part].at[net.at(dim, 2), pl.ds(2 * half, 2)],
                    relay_in[part].at[half],
                    net.peer(dim, delta),
                )
            )
            early[part].append(
                net.send(
                    first[part].at[net.at(dim, delta), pl.ds(2 - 2 * half, 2)],
                    first_in[part].at[half, pl.ds(2 - 2 * half, 2)],
                    net.peer(dim, delta),
                )
            )

    def passed(part):
        finish(flights[part])
        dim = ORDERS[part][0]
        for half, delta in ((0, 1), (1, 3)):
            there = net.at(dim, delta)
            for a in range(2):
                row = 2 * half + a
                value = f32(first[part][there, row]) + f32(relay_in[part][half, a])
                first[part][there, row] = value.astype(BF16)
            flights[part].append(
                net.send(
                    first[part].at[there, pl.ds(2 * half, 2)],
                    first_in[part].at[half, pl.ds(2 * half, 2)],
                    net.peer(dim, delta),
                )
            )

    def push(part, step, source, target):
        dim = ORDERS[part][step]
        for delta in (2, 1, 3):
            flights[part].append(
                net.send(source.at[net.at(dim, delta)], target.at[delta - 1], net.peer(dim, delta))
            )

    def summed(part):
        finish(flights[part])
        finish(early[part])
        mine = net.coords[ORDERS[part][0]]
        for a in range(RING):
            value = f32(first[part][mine, a])
            value = value + (f32(first_in[part][0, a]) + f32(first_in[part][1, a]))
            second[part][a] = value.astype(BF16)
        push(part, 1, second[part], second_in[part])

    def summed_again(part):
        finish(flights[part])
        mine = net.coords[ORDERS[part][1]]
        value = f32(second[part][mine]) + f32(second_in[part][0])
        value = value + (f32(second_in[part][1]) + f32(second_in[part][2]))
        third[part][...] = value.astype(BF16)
        push(part, 2, third[part], third_in[part])

    def summed_last(part):
        low, size = SCATTER_CUTS[part]
        finish(flights[part])
        mine = net.coords[ORDERS[part][2]]
        value = f32(third[part][mine]) + f32(third_in[part][0])
        value = value + (f32(third_in[part][1]) + f32(third_in[part][2]))
        weight_grad[:, pl.ds(low, size)] = value

    def gain_round(dim, value):
        gain_sum[dim + 1] = value
        gain_in[dim, net.coords[dim]] = value
        return [
            net.send(
                gain_sum.at[dim + 1], gain_in.at[dim, net.coords[dim]], net.peer(dim, delta)
            )
            for delta in range(1, RING)
        ]

    def gain_total(dim, copies):
        finish(copies)
        return (gain_in[dim, 0] + gain_in[dim, 1]) + (gain_in[dim, 2] + gain_in[dim, 3])

    out_copies = []

    def input_grad(i):
        rows = pl.ds(i * TILE, TILE)
        weight = kv[...].reshape(WIDTH, 2 * WIDTH)
        tall = lax.broadcasted_iota(jnp.int32, (TILE, HEAD_WIDTH), 0) + i * TILE
        hot = jnp.where(tall == lane_last[:1], 1.0, 0.0).astype(BF16)
        grad_normed = dot(both[rows, :], weight, 1, 1) + dot(hot, select_rows[...])
        inv = inv_s[rows, :]
        normed = f32(hid[pl.ds(i * blocks, blocks)]).reshape(TILE, WIDTH) * inv
        scaled = grad_normed * gain
        mean = jnp.mean(scaled * normed, axis=-1, keepdims=True)
        value = inv * (scaled - normed * mean) + dot(hot, pool_rows[...])
        result[rows, :] = value.astype(BF16)
        out_copies.append(net.local(result.at[rows], grad_in.at[rows]))

    pairs = [share_part(0), share_part(1)]
    halves(0)
    pairs.append(share_part(2))
    halves(1)
    for g in range(KEY_HEADS):
        flatten(g, dot(gscore[pair_rows(g), :], joint[:, head(g)]))
    query_back = dot(flat[...].astype(BF16), wq[...], 1, 1)
    select_rows[...] = three(query_back)
    gain_part = jnp.sum(gain_acc[...].T, axis=0, keepdims=True) / gain
    gain_part = gain_part + jnp.sum(query_back * normed_last, axis=0, keepdims=True)
    gain_sum[0] = gain_part
    gain_copies = [net.send(gain_sum.at[0], gain_pair, net.sibling)]
    halves(2)
    passed(0)
    input_grad(0)
    finish(gain_copies)
    gain_copies = gain_round(0, gain_sum[0] + gain_pair[...])
    passed(1)
    passed(2)
    summed(0)
    input_grad(1)
    gain_copies = gain_round(1, gain_total(0, gain_copies))
    summed(1)
    summed(2)
    summed_again(0)
    input_grad(2)
    gain_copies = gain_round(2, gain_total(1, gain_copies))
    summed_again(1)
    summed_again(2)
    input_grad(3)
    gain_grad[...] = gain_total(2, gain_copies)
    for part in range(3):
        summed_last(part)
    finish(out_copies)


def per_device(
    hidden_in, lengths, owner, pooled_grad, norm_gain, w_query, w_key, value_weight, w_out
):
    tokens, width = hidden_in.shape
    heads = QUERY_HEADS * SLOTS
    grid = (RING, RING, RING, 2, SLOTS)

    def vmem(*shape, kind=BF16):
        return pltpu.VMEM(shape, kind)

    def parts(*lead):
        return [vmem(*lead, SLOTS, size) for _, size in SCATTER_CUTS]

    spec = pl.BlockSpec(memory_space=pltpu.VMEM)
    smem = pl.BlockSpec(memory_space=pltpu.SMEM)
    hbm = pl.BlockSpec(memory_space=pl.ANY)
    grad_in, weight_grad, gain_grad = pl.pallas_call(
        step_kernel,
        out_shape=(
            jax.ShapeDtypeStruct((tokens, width), BF16),
            jax.ShapeDtypeStruct((SLOTS, 2 * WIDTH), F32),
            jax.ShapeDtypeStruct((1, width), F32),
        ),
        in_specs=[smem, smem, hbm, spec, spec, hbm, spec, spec, hbm],
        out_specs=(hbm, spec, spec),
        scratch_shapes=[
            vmem(tokens // SLOTS, SLOTS, width),
            vmem(width, 2 * WIDTH),
            vmem(2 * WIDTH, width),
            vmem(*grid, 2 * WIDTH),
            vmem(*grid, width),
            vmem(SLOTS, width),
            vmem(tokens, width),
            vmem(width, tokens),
            vmem(tokens, 1, kind=F32),
            vmem(tokens, 2 * WIDTH),
            vmem(tokens, 2 * WIDTH),
            vmem(tokens, width),
            vmem(heads, tokens, kind=F32),
            vmem(heads, tokens, kind=F32),
            vmem(heads, tokens),
            vmem(heads, HEAD_WIDTH, kind=F32),
            vmem(heads, HEAD_WIDTH, kind=F32),
            vmem(SLOTS, 2 * WIDTH, kind=F32),
            vmem(SLOTS, 2 * WIDTH),
            vmem(HEAD_WIDTH, width),
            vmem(HEAD_WIDTH, width),
            vmem(*grid, 2 * WIDTH),
            vmem(width, HEAD_WIDTH, kind=F32),
            vmem(1, width, kind=F32),
            vmem(4, 1, width, kind=F32),
            vmem(3, RING, 1, width, kind=F32),
            pltpu.SemaphoreType.DMA((2, 256)),
        ]
        + parts(RING, RING, RING)
        + parts(RING, RING, RING)
        + parts(2, 2, RING)
        + parts(2, RING, RING)
        + parts(RING, RING)
        + parts(RING - 1, RING)
        + parts(RING)
        + parts(RING - 1),
        compiler_params=pltpu.CompilerParams(
            collective_id=0, has_side_effects=True, vmem_limit_bytes=60 * 2**20
        ),
        name="step",
    )(
        lengths,
        owner,
        hidden_in.reshape(tokens // SLOTS, SLOTS, width),
        pooled_grad,
        norm_gain.reshape(1, width),
        w_query,
        w_key,
        value_weight,
        w_out,
    )
    return grad_in, weight_grad[:, :WIDTH], weight_grad[:, WIDTH:], gain_grad.reshape(-1)


def solution(mesh):
    return jax.shard_map(
        per_device,
        mesh=mesh,
        in_specs=(
            P("dp", None),
            P("dp", None),
            P("dp"),
            P("dp", None),
            P(),
            P(),
            P("dp", None),
            P("dp", None),
            P(),
        ),
        out_specs=(P("dp", None), P("dp", None), P("dp", None), P()),
        check_vma=False,
    )
```

```python
import functools
import jax
import jax.numpy as jnp
from jax import lax
from jax.experimental import pallas as pl
from jax.experimental.pallas import tpu as pltpu
from jax.sharding import PartitionSpec as P

QUERY_HEADS = 16
KEY_HEADS = 8
HEAD_WIDTH = 128
WIDTH = KEY_HEADS * HEAD_WIDTH
SLOTS = 8
TILE = 256
RING = 4
STRIDES = (32, 8, 2)
ORDERS = ((0, 1, 2), (1, 2, 0), (2, 0, 1))
MESH = pl.DeviceIdType.MESH
BF16, F32 = jnp.bfloat16, jnp.float32
GATHER_CUTS = (
    ((0, 384), (384, 384), (768, 256)),
    ((0, 256), (256, 384), (640, 384)),
    ((0, 384), (384, 256), (640, 384)),
)
SCATTER_CUTS = ((0, 768), (768, 640), (1408, 640))


def f32(value):
    return value.astype(F32)


def dot(a, b, ca=1, cb=0):
    return lax.dot_general(a, b, (((ca,), (cb,)), ((), ())), preferred_element_type=F32)


class Net:
    def __init__(self, sems):
        self.sems, self.used = sems, 0
        me = lax.axis_index("dp")
        self.me = me
        self.coords = ((me // 32) % RING, (me // 8) % RING, (me // 2) % RING)
        self.core = me % 2
        self.sibling = me + 1 - 2 * self.core

    def at(self, dim, delta):
        return (self.coords[dim] + delta + RING) % RING

    def peer(self, dim, delta):
        return self.me + (self.at(dim, delta) - self.coords[dim]) * STRIDES[dim]

    def greet(self):
        barrier = pltpu.get_barrier_semaphore()
        pl.semaphore_signal(barrier, inc=1, device_id=(self.sibling,), device_id_type=MESH)
        for dim in range(3):
            for delta in range(1, RING):
                pl.semaphore_signal(
                    barrier, inc=1, device_id=(self.peer(dim, delta),), device_id_type=MESH
                )
        pl.semaphore_wait(barrier, 10)

    def send(self, src, dst, other):
        copy = pltpu.make_async_remote_copy(
            src_ref=src,
            dst_ref=dst,
            send_sem=self.sems.at[0, self.used],
            recv_sem=self.sems.at[1, self.used],
            device_id=(other,),
            device_id_type=MESH,
        )
        self.used += 1
        copy.start()
        return copy

    def local(self, src, dst):
        copy = pltpu.make_async_copy(src, dst, self.sems.at[0, self.used])
        self.used += 1
        copy.start()
        return copy


def finish(copies):
    for copy in copies:
        copy.wait()
    copies.clear()


class Gather:
    def __init__(self, net, source, target, low, size, order):
        self.net, self.order = net, order
        self.source = source.at[:, pl.ds(low, size)]
        self.target = target.at[:, :, :, :, :, pl.ds(low, size)]
        self.flying, self.paired = [], []

    def slab(self, done, dim=None, delta=0, half=None):
        net = self.net
        index = [net.coords[0], net.coords[1], net.coords[2], net.core]
        if dim is not None:
            index[dim] = net.at(dim, delta)
        for at in done:
            index[at] = slice(None)
        if half is not None:
            index[done[0]] = pl.ds(half * 2, 2)
        return self.target.at[tuple(index)]

    def open(self):
        net, mine = self.net, self.slab(())
        self.own = net.local(self.source, mine)
        for delta in (2, 1, 3):
            self.flying.append(net.send(self.source, mine, net.peer(self.order[0], delta)))

    def pair(self, step, delta):
        piece = self.slab(self.order[:step], self.order[step], delta)
        self.paired.append(self.net.send(piece, piece, self.net.sibling))

    def ring(self, step):
        if step == 1:
            self.own.wait()
        finish(self.flying)
        dim, piece = self.order[step], self.slab(self.order[:step])
        for delta in (2, 1, 3):
            self.flying.append(self.net.send(piece, piece, self.net.peer(dim, delta)))
        if step == 2:
            self.pair(2, 0)

    def relay(self, step):
        if step == 2:
            self.flying[1].wait()
            self.pair(2, 3)
            self.flying[2].wait()
            self.pair(2, 1)

    def close(self):
        self.flying[0].wait()
        self.pair(2, 2)


def step_kernel(
    lengths_hbm,
    owner_hbm,
    hidden_hbm,
    grad_hbm,
    gain_hbm,
    query_hbm,
    key_hbm,
    value_hbm,
    out_hbm,
    grad_in,
    packed,
    *scratch,
):
    (hid, wq, wo, kv, every, grad_b, nb, nbt, inv_s, joint, both, result) = scratch[:12]
    (score, prob, gscore, q_all, a_all, flat, flat_b, select_rows, pool_rows) = scratch[12:21]
    (share, gain_acc, gain_pair, gain_sum, gain_in, sems) = scratch[21:27]
    pair_in, first, relay_in, first_in, second, second_in, third, third_in = (
        scratch[27 + 3 * i : 30 + 3 * i] for i in range(8)
    )
    lengths, owner, grad_f, gain_ref, key_ref, value_ref, hid_sems = scratch[51:]
    net = Net(sems)
    scale_q = 1.0 / HEAD_WIDTH**0.5
    tokens = nb.shape[0]
    tiles = tokens // TILE
    blocks = TILE // SLOTS

    key_copy = net.local(key_hbm, key_ref)
    value_copy = net.local(value_hbm, value_ref)
    grad_copy = net.local(grad_hbm, grad_f)
    small = [
        net.local(gain_hbm, gain_ref),
        net.local(lengths_hbm, lengths),
        net.local(owner_hbm, owner),
    ]

    def hid_copy(i):
        part = pl.ds(i * blocks, blocks)
        return pltpu.make_async_copy(hidden_hbm.at[part], hid.at[part], hid_sems.at[i])

    for i in range(tiles):
        hid_copy(i).start()

    def load(src, dst):
        rows = dst.shape[0] // 4
        return [
            net.local(src.at[pl.ds(n * rows, rows)], dst.at[pl.ds(n * rows, rows)])
            for n in range(4)
        ]

    net.greet()
    key_parts, value_parts, grad_parts = (
        [
            Gather(net, source, target, low, size, ORDERS[part])
            for part, (low, size) in enumerate(cuts)
        ]
        for source, target, cuts in (
            (key_ref, kv.at[:, :, :, :, :, pl.ds(0, WIDTH)], GATHER_CUTS[0]),
            (value_ref, kv.at[:, :, :, :, :, pl.ds(WIDTH, WIDTH)], GATHER_CUTS[1]),
            (grad_b, every, GATHER_CUTS[2]),
        )
    )
    key_copy.wait()
    for part in key_parts:
        part.open()
    value_copy.wait()
    for part in value_parts:
        part.open()
    grad_copy.wait()
    grad_b[...] = grad_f[...].astype(BF16)
    for part in grad_parts:
        part.open()
    finish(small)
    gain = f32(gain_ref[...]).reshape(1, WIDTH)

    def norm_tile(i):
        hid_copy(i).wait()
        rows = pl.ds(pl.multiple_of(i * TILE, TILE), TILE)
        x = f32(hid[pl.ds(i * blocks, blocks)]).reshape(TILE, WIDTH)
        inv = lax.rsqrt(jnp.mean(x * x, axis=-1, keepdims=True) + 1e-06)
        inv_s[rows, :] = inv
        y = (x * inv) * gain
        nb[rows, :] = y.astype(BF16)
        nbt[:, rows] = y.T.astype(BF16)

    @pl.loop(0, tiles // 2)
    def _(i):
        norm_tile(i)

    for part in key_parts:
        part.ring(1)
    for part in value_parts:
        part.ring(1)

    @pl.loop(tiles // 2, tiles)
    def _(i):
        norm_tile(i)

    wq_copy = load(query_hbm, wq)
    for part in key_parts:
        part.ring(2)
    for part in value_parts:
        part.ring(2)
    for part in grad_parts:
        part.ring(1)

    row8 = lax.broadcasted_iota(jnp.int32, (SLOTS, WIDTH), 0)
    lane = lax.broadcasted_iota(jnp.int32, (SLOTS, WIDTH), 1)
    starts = jnp.zeros((SLOTS, WIDTH), jnp.int32)
    ends = jnp.zeros((SLOTS, WIDTH), jnp.int32)
    lane_last = jnp.full((SLOTS, HEAD_WIDTH), -1, jnp.int32)
    short_lane = lax.broadcasted_iota(jnp.int32, (SLOTS, HEAD_WIDTH), 1)
    hidden_last = jnp.zeros((SLOTS, WIDTH), F32)
    at = jnp.int32(0)
    for s in range(SLOTS):
        starts = jnp.where(row8 == s, at, starts)
        at = at + lengths[0, s]
        ends = jnp.where(row8 == s, at, ends)
        last = jnp.maximum(at - 1, 0)
        chosen = (short_lane % SLOTS == s) & (short_lane < 3 * SLOTS)
        lane_last = jnp.where(chosen, last, lane_last)
        block = f32(hid[last // SLOTS])
        picked = jnp.sum(jnp.where(row8 == last % SLOTS, block, 0.0), axis=0, keepdims=True)
        hidden_last = jnp.where(row8 == s, picked, hidden_last)
    member = (lane >= starts) & (lane < ends)
    inv_last = lax.rsqrt(jnp.mean(hidden_last * hidden_last, axis=-1, keepdims=True) + 1e-06)
    normed_last = hidden_last * inv_last
    last_b = (normed_last * gain).astype(BF16)

    finish(wq_copy)

    def spread(value, at, target):
        for part in range(value.shape[1] // HEAD_WIDTH):
            target[pl.ds(SLOTS * (at + part), SLOTS), :] = f32(
                value[:, part * HEAD_WIDTH : (part + 1) * HEAD_WIDTH].astype(BF16)
            )

    for n in range(4):
        spread(dot(last_b, wq[:, pl.ds(512 * n, 512)]), 4 * n, q_all)
    for part in key_parts:
        part.relay(2)
    for part in grad_parts:
        part.ring(2)
    for part in key_parts:
        part.close()
    for part in value_parts:
        part.relay(2)
    wo_copy = load(out_hbm, wo)
    for part in key_parts:
        finish(part.paired)

    def project(i, low):
        rows = pl.ds(pl.multiple_of(i * TILE, TILE), TILE)
        weight = kv[:, :, :, :, :, pl.ds(low, WIDTH)].reshape(WIDTH, WIDTH)
        joint[rows, pl.ds(low, WIDTH)] = dot(nb[rows, :], weight).astype(BF16)

    @pl.loop(0, tiles // 2)
    def _(i):
        project(i, 0)

    for part in value_parts:
        part.close()

    @pl.loop(tiles // 2, tiles)
    def _(i):
        project(i, 0)

    for part in value_parts:
        finish(part.paired)
    for part in grad_parts:
        part.relay(2)

    @pl.loop(0, tiles)
    def _(i):
        project(i, WIDTH)

    for part in grad_parts:
        part.close()

    def head(g, base=0):
        return pl.ds(base + g * HEAD_WIDTH, HEAD_WIDTH)

    def pair_rows(g):
        return pl.ds(2 * SLOTS * g, 2 * SLOTS)

    for g in range(KEY_HEADS):
        score[pair_rows(g), :] = dot(q_all[pair_rows(g), :].astype(BF16), joint[:, head(g)], 1, 1)
    scores = score[...].reshape(QUERY_HEADS, SLOTS, tokens) * scale_q
    scores = jnp.where(member[None], scores, -1e30)
    expo = jnp.exp(scores - jnp.max(scores, axis=-1, keepdims=True))
    probs = expo / jnp.sum(expo, axis=-1, keepdims=True)
    prob[...] = probs.reshape(QUERY_HEADS * SLOTS, tokens)

    def flatten(g, value):
        for q in range(2):
            flat[:, head(2 * g + q)] = value[q * SLOTS : (q + 1) * SLOTS, :]

    for g in range(KEY_HEADS):
        flatten(g, dot(prob[pair_rows(g), :].astype(BF16), joint[:, head(g, WIDTH)]))
    finish(wo_copy)
    pooled = hidden_last + dot(flat[...].astype(BF16), wo[...])
    for part in grad_parts:
        finish(part.paired)
    cached = jnp.zeros((SLOTS, WIDTH), F32)
    for s in range(SLOTS):
        o = owner[s]
        block = f32(every[o // 256, (o // 64) % RING, (o // 16) % RING, (o // 8) % 2])
        picked = jnp.sum(jnp.where(row8 == o % SLOTS, block, 0.0), axis=0, keepdims=True)
        cached = jnp.where(row8 == s, picked, cached)
    inv_len = lax.rsqrt(jnp.sum(pooled * pooled, axis=-1, keepdims=True) + 1e-06)
    embed = pooled * inv_len
    grad_pool = inv_len * (cached - embed * jnp.sum(embed * cached, axis=-1, keepdims=True))
    grad_pool_b = grad_pool.astype(BF16)
    for n in range(4):
        spread(dot(grad_pool_b, wo[pl.ds(512 * n, 512), :], 1, 1), 4 * n, a_all)

    def three(value):
        hi = f32(value.astype(BF16))
        mid = f32((value - hi).astype(BF16))
        rest = jnp.zeros((HEAD_WIDTH - 3 * SLOTS, WIDTH), F32)
        return jnp.concatenate([hi, mid, (value - hi) - mid, rest], axis=0).astype(BF16)

    pool_rows[...] = three(grad_pool)

    for g in range(KEY_HEADS):
        score[pair_rows(g), :] = dot(
            a_all[pair_rows(g), :].astype(BF16), joint[:, head(g, WIDTH)], 1, 1
        )
        both[:, head(g, WIDTH)] = dot(
            prob[pair_rows(g), :].astype(BF16), a_all[pair_rows(g), :].astype(BF16), 0, 0
        ).astype(BF16)
    grad_prob = score[...]
    probs = prob[...]
    inner = jnp.sum(probs * grad_prob, axis=-1, keepdims=True)
    gscore[...] = (probs * (grad_prob - inner) * scale_q).astype(BF16)
    for g in range(KEY_HEADS):
        both[:, head(g)] = dot(
            gscore[pair_rows(g), :], q_all[pair_rows(g), :].astype(BF16), 0, 0
        ).astype(BF16)

    def share_part(part):
        low, size = SCATTER_CUTS[part]

        @pl.loop(0, RING)
        def _(x):
            rows = pl.ds(pl.multiple_of(x * TILE, TILE), TILE)
            value = dot(nbt[rows, :], both[:, pl.ds(low, size)])
            share[x, :, :, :, :, pl.ds(low, size)] = value.reshape(
                RING, RING, 2, SLOTS, size
            ).astype(BF16)
            weight = f32(kv[x, :, :, :, :, pl.ds(low, size)]).reshape(TILE, size)
            product = value * weight
            total = product[:, :HEAD_WIDTH]
            for n in range(1, size // HEAD_WIDTH):
                total = total + product[:, n * HEAD_WIDTH : (n + 1) * HEAD_WIDTH]
            if part == 0:
                gain_acc[rows, :] = total
            else:
                gain_acc[rows, :] += total

        return net.send(
            share.at[:, :, :, 1 - net.core, :, pl.ds(low, size)], pair_in[part], net.sibling
        )

    flights = [[], [], []]
    early = [[], [], []]

    def halves(part):
        pairs[part].wait()
        low, size = SCATTER_CUTS[part]
        order = ORDERS[part]

        @pl.loop(0, RING * RING)
        def _(at):
            ahead = [at // RING, at % RING, 0]
            for z in range(RING):
                ahead[2] = z
                value = f32(share[ahead[0], ahead[1], z, net.core, :, pl.ds(low, size)])
                value = value + f32(pair_in[part][ahead[0], ahead[1], z])
                first[part][ahead[order[0]], ahead[order[1]], ahead[order[2]]] = value.astype(BF16)

        dim = order[0]
        for half, delta in ((0, 1), (1, 3)):
            flights[part].append(
                net.send(
                    first[part].at[net.at(dim, 2), pl.ds(2 * half, 2)],
                    relay_in[part].at[half],
                    net.peer(dim, delta),
                )
            )
            early[part].append(
                net.send(
                    first[part].at[net.at(dim, delta), pl.ds(2 - 2 * half, 2)],
                    first_in[part].at[half, pl.ds(2 - 2 * half, 2)],
                    net.peer(dim, delta),
                )
            )

    def passed(part):
        finish(flights[part])
        dim = ORDERS[part][0]
        for half, delta in ((0, 1), (1, 3)):
            there = net.at(dim, delta)
            for a in range(2):
                row = 2 * half + a
                value = f32(first[part][there, row]) + f32(relay_in[part][half, a])
                first[part][there, row] = value.astype(BF16)
            flights[part].append(
                net.send(
                    first[part].at[there, pl.ds(2 * half, 2)],
                    first_in[part].at[half, pl.ds(2 * half, 2)],
                    net.peer(dim, delta),
                )
            )

    def push(part, step, source, target):
        dim = ORDERS[part][step]
        for delta in (2, 1, 3):
            flights[part].append(
                net.send(source.at[net.at(dim, delta)], target.at[delta - 1], net.peer(dim, delta))
            )

    def summed(part):
        finish(flights[part])
        finish(early[part])
        mine = net.coords[ORDERS[part][0]]
        for a in range(RING):
            value = f32(first[part][mine, a])
            value = value + (f32(first_in[part][0, a]) + f32(first_in[part][1, a]))
            second[part][a] = value.astype(BF16)
        push(part, 1, second[part], second_in[part])

    def summed_again(part):
        finish(flights[part])
        mine = net.coords[ORDERS[part][1]]
        value = f32(second[part][mine]) + f32(second_in[part][0])
        value = value + (f32(second_in[part][1]) + f32(second_in[part][2]))
        third[part][...] = value.astype(BF16)
        push(part, 2, third[part], third_in[part])

    def summed_last(part):
        low, size = SCATTER_CUTS[part]
        finish(flights[part])
        mine = net.coords[ORDERS[part][2]]
        value = f32(third[part][mine]) + f32(third_in[part][0])
        value = value + (f32(third_in[part][1]) + f32(third_in[part][2]))
        packed[:SLOTS, pl.ds(low, size)] = value

    def gain_round(dim, value):
        gain_sum[dim + 1] = value
        gain_in[dim, net.coords[dim]] = value
        return [
            net.send(
                gain_sum.at[dim + 1], gain_in.at[dim, net.coords[dim]], net.peer(dim, delta)
            )
            for delta in range(1, RING)
        ]

    def gain_total(dim, copies):
        finish(copies)
        return (gain_in[dim, 0] + gain_in[dim, 1]) + (gain_in[dim, 2] + gain_in[dim, 3])

    out_copies = []

    def input_grad(i):
        rows = pl.ds(i * TILE, TILE)
        weight = kv[...].reshape(WIDTH, 2 * WIDTH)
        tall = lax.broadcasted_iota(jnp.int32, (TILE, HEAD_WIDTH), 0) + i * TILE
        hot = jnp.where(tall == lane_last[:1], 1.0, 0.0).astype(BF16)
        grad_normed = dot(both[rows, :], weight, 1, 1) + dot(hot, select_rows[...])
        inv = inv_s[rows, :]
        normed = f32(hid[pl.ds(i * blocks, blocks)]).reshape(TILE, WIDTH) * inv
        scaled = grad_normed * gain
        mean = jnp.mean(scaled * normed, axis=-1, keepdims=True)
        value = inv * (scaled - normed * mean) + dot(hot, pool_rows[...])
        result[rows, :] = value.astype(BF16)
        out_copies.append(net.local(result.at[rows], grad_in.at[rows]))

    pairs = [share_part(0), share_part(1)]
    halves(0)
    pairs.append(share_part(2))
    halves(1)
    for g in range(KEY_HEADS):
        flatten(g, dot(gscore[pair_rows(g), :], joint[:, head(g)]))
    query_back = dot(flat[...].astype(BF16), wq[...], 1, 1)
    select_rows[...] = three(query_back)
    gain_part = jnp.sum(gain_acc[...].T, axis=0, keepdims=True) / gain
    gain_part = gain_part + jnp.sum(query_back * normed_last, axis=0, keepdims=True)
    gain_sum[0] = gain_part
    gain_copies = [net.send(gain_sum.at[0], gain_pair, net.sibling)]
    halves(2)
    passed(0)
    input_grad(0)
    finish(gain_copies)
    gain_copies = gain_round(0, gain_sum[0] + gain_pair[...])
    passed(1)
    passed(2)
    summed(0)
    input_grad(1)
    gain_copies = gain_round(1, gain_total(0, gain_copies))
    summed(1)
    summed(2)
    summed_again(0)
    input_grad(2)
    gain_copies = gain_round(2, gain_total(1, gain_copies))
    summed_again(1)
    summed_again(2)
    input_grad(3)
    packed[SLOTS : SLOTS + 1, :WIDTH] = gain_total(2, gain_copies)
    for part in range(3):
        summed_last(part)
    finish(out_copies)


def per_device(
    hidden_in, lengths, owner, pooled_grad, norm_gain, w_query, w_key, value_weight, w_out
):
    tokens, width = hidden_in.shape
    heads = QUERY_HEADS * SLOTS
    grid = (RING, RING, RING, 2, SLOTS)

    def vmem(*shape, kind=BF16):
        return pltpu.VMEM(shape, kind)

    def parts(*lead):
        return [vmem(*lead, SLOTS, size) for _, size in SCATTER_CUTS]

    spec = pl.BlockSpec(memory_space=pltpu.VMEM)
    hbm = pl.BlockSpec(memory_space=pltpu.HBM)
    whole = pl.BlockSpec(memory_space=pl.ANY)
    grad_in, packed = pl.pallas_call(
        step_kernel,
        out_shape=(
            jax.ShapeDtypeStruct((tokens, width), BF16),
            jax.ShapeDtypeStruct((2 * SLOTS, 2 * WIDTH), F32),
        ),
        in_specs=[hbm] * 9,
        out_specs=(whole, spec),
        scratch_shapes=[
            vmem(tokens // SLOTS, SLOTS, width),
            vmem(width, 2 * WIDTH),
            vmem(2 * WIDTH, width),
            vmem(*grid, 2 * WIDTH),
            vmem(*grid, width),
            vmem(SLOTS, width),
            vmem(tokens, width),
            vmem(width, tokens),
            vmem(tokens, 1, kind=F32),
            vmem(tokens, 2 * WIDTH),
            vmem(tokens, 2 * WIDTH),
            vmem(tokens, width),
            vmem(heads, tokens, kind=F32),
            vmem(heads, tokens, kind=F32),
            vmem(heads, tokens),
            vmem(heads, HEAD_WIDTH, kind=F32),
            vmem(heads, HEAD_WIDTH, kind=F32),
            vmem(SLOTS, 2 * WIDTH, kind=F32),
            vmem(SLOTS, 2 * WIDTH),
            vmem(HEAD_WIDTH, width),
            vmem(HEAD_WIDTH, width),
            vmem(*grid, 2 * WIDTH),
            vmem(width, HEAD_WIDTH, kind=F32),
            vmem(1, width, kind=F32),
            vmem(4, 1, width, kind=F32),
            vmem(3, RING, 1, width, kind=F32),
            pltpu.SemaphoreType.DMA((2, 256)),
        ]
        + parts(RING, RING, RING)
        + parts(RING, RING, RING)
        + parts(2, 2, RING)
        + parts(2, RING, RING)
        + parts(RING, RING)
        + parts(RING - 1, RING)
        + parts(RING)
        + parts(RING - 1)
        + [
            pltpu.SMEM((1, SLOTS), jnp.int32),
            pltpu.SMEM((SLOTS,), jnp.int32),
            vmem(SLOTS, width, kind=F32),
            vmem(width),
            vmem(SLOTS, WIDTH),
            vmem(SLOTS, WIDTH),
            pltpu.SemaphoreType.DMA((tokens // TILE,)),
        ],
        compiler_params=pltpu.CompilerParams(
            collective_id=0, has_side_effects=True, vmem_limit_bytes=50 * 2**20
        ),
        name="step",
    )(
        *(
            pltpu.with_memory_space_constraint(value, pltpu.HBM)
            for value in (
                lengths,
                owner,
                hidden_in.reshape(tokens // SLOTS, SLOTS, width),
                pooled_grad,
                norm_gain,
                w_query,
                w_key,
                value_weight,
                w_out,
            )
        )
    )
    return grad_in, packed[:SLOTS, :WIDTH], packed[:SLOTS, WIDTH:], packed[SLOTS, :WIDTH]


def solution(mesh):
    return jax.shard_map(
        per_device,
        mesh=mesh,
        in_specs=(
            P("dp", None),
            P("dp", None),
            P("dp"),
            P("dp", None),
            P(),
            P(),
            P("dp", None),
            P("dp", None),
            P(),
        ),
        out_specs=(P("dp", None), P("dp", None), P("dp", None), P()),
        check_vma=False,
    )
```

```python
import functools
import jax
import jax.numpy as jnp
from jax import lax
from jax.experimental import pallas as pl
from jax.experimental.pallas import tpu as pltpu
from jax.sharding import PartitionSpec as P

QUERY_HEADS = 16
KEY_HEADS = 8
HEAD_WIDTH = 128
WIDTH = KEY_HEADS * HEAD_WIDTH
SLOTS = 8
TILE = 256
RING = 4
STRIDES = (32, 8, 2)
ORDERS = ((0, 1, 2), (1, 2, 0), (2, 0, 1))
MESH = pl.DeviceIdType.MESH
BF16, F32 = jnp.bfloat16, jnp.float32
GATHER_CUTS = (
    ((0, 384), (384, 384), (768, 256)),
    ((0, 256), (256, 384), (640, 384)),
    ((0, 384), (384, 256), (640, 384)),
)
SCATTER_CUTS = ((0, 768), (768, 768), (1536, 512))


def f32(value):
    return value.astype(F32)


def dot(a, b, ca=1, cb=0):
    return lax.dot_general(a, b, (((ca,), (cb,)), ((), ())), preferred_element_type=F32)


class Net:
    def __init__(self, sems):
        self.sems, self.used = sems, 0
        me = lax.axis_index("dp")
        self.me = me
        self.coords = ((me // 32) % RING, (me // 8) % RING, (me // 2) % RING)
        self.core = me % 2
        self.sibling = me + 1 - 2 * self.core

    def at(self, dim, delta):
        return (self.coords[dim] + delta + RING) % RING

    def peer(self, dim, delta):
        return self.me + (self.at(dim, delta) - self.coords[dim]) * STRIDES[dim]

    def greet(self):
        barrier = pltpu.get_barrier_semaphore()
        pl.semaphore_signal(barrier, inc=1, device_id=(self.sibling,), device_id_type=MESH)
        for dim in range(3):
            for delta in range(1, RING):
                pl.semaphore_signal(
                    barrier, inc=1, device_id=(self.peer(dim, delta),), device_id_type=MESH
                )
        pl.semaphore_wait(barrier, 10)

    def send(self, src, dst, other):
        copy = pltpu.make_async_remote_copy(
            src_ref=src,
            dst_ref=dst,
            send_sem=self.sems.at[0, self.used],
            recv_sem=self.sems.at[1, self.used],
            device_id=(other,),
            device_id_type=MESH,
        )
        self.used += 1
        copy.start()
        return copy

    def local(self, src, dst):
        copy = pltpu.make_async_copy(src, dst, self.sems.at[0, self.used])
        self.used += 1
        copy.start()
        return copy


def finish(copies):
    for copy in copies:
        copy.wait()
    copies.clear()


class Gather:
    def __init__(self, net, source, target, low, size, order):
        self.net, self.order = net, order
        self.source = source.at[:, pl.ds(low, size)]
        self.target = target.at[:, :, :, :, :, pl.ds(low, size)]
        self.flying, self.paired = [], []

    def slab(self, done, dim=None, delta=0, half=None):
        net = self.net
        index = [net.coords[0], net.coords[1], net.coords[2], net.core]
        if dim is not None:
            index[dim] = net.at(dim, delta)
        for at in done:
            index[at] = slice(None)
        if half is not None:
            index[done[0]] = pl.ds(half * 2, 2)
        return self.target.at[tuple(index)]

    def open(self):
        net, mine = self.net, self.slab(())
        self.own = net.local(self.source, mine)
        for delta in (2, 1, 3):
            self.flying.append(net.send(self.source, mine, net.peer(self.order[0], delta)))

    def pair(self, step, delta):
        piece = self.slab(self.order[:step], self.order[step], delta)
        self.paired.append(self.net.send(piece, piece, self.net.sibling))

    def ring(self, step):
        if step == 1:
            self.own.wait()
        finish(self.flying)
        dim, piece = self.order[step], self.slab(self.order[:step])
        for delta in (2, 1, 3):
            self.flying.append(self.net.send(piece, piece, self.net.peer(dim, delta)))
        if step == 2:
            self.pair(2, 0)

    def relay(self, step):
        if step == 2:
            self.flying[1].wait()
            self.pair(2, 3)
            self.flying[2].wait()
            self.pair(2, 1)

    def close(self):
        self.flying[0].wait()
        self.pair(2, 2)


def step_kernel(
    lengths_hbm,
    owner_hbm,
    hidden_hbm,
    grad_hbm,
    gain_hbm,
    query_hbm,
    key_hbm,
    value_hbm,
    out_hbm,
    grad_in,
    packed,
    *scratch,
):
    (hid, wq, wo, kv, every, grad_b, nb, nbt, inv_s, joint, both, result) = scratch[:12]
    (score, prob, gscore, q_all, a_all, flat, flat_b, select_rows, pool_rows) = scratch[12:21]
    (share, gain_acc, gain_pair, gain_sum, gain_in, sems) = scratch[21:27]
    pair_in, first, relay_in, first_in, second, second_in, third, third_in = (
        scratch[27 + 3 * i : 30 + 3 * i] for i in range(8)
    )
    lengths, owner, grad_f, gain_ref, key_ref, value_ref, hid_sems = scratch[51:]
    net = Net(sems)
    scale_q = 1.0 / HEAD_WIDTH**0.5
    tokens = nb.shape[0]
    tiles = tokens // TILE
    blocks = TILE // SLOTS

    key_copy = net.local(key_hbm, key_ref)
    value_copy = net.local(value_hbm, value_ref)
    grad_copy = net.local(grad_hbm, grad_f)
    small = [
        net.local(gain_hbm, gain_ref),
        net.local(lengths_hbm, lengths),
        net.local(owner_hbm, owner),
    ]

    def hid_copy(i):
        part = pl.ds(i * blocks, blocks)
        return pltpu.make_async_copy(hidden_hbm.at[part], hid.at[part], hid_sems.at[i])

    for i in range(tiles):
        hid_copy(i).start()

    def load(src, dst):
        rows = dst.shape[0] // 4
        return [
            net.local(src.at[pl.ds(n * rows, rows)], dst.at[pl.ds(n * rows, rows)])
            for n in range(4)
        ]

    net.greet()
    key_parts, value_parts, grad_parts = (
        [
            Gather(net, source, target, low, size, ORDERS[part])
            for part, (low, size) in enumerate(cuts)
        ]
        for source, target, cuts in (
            (key_ref, kv.at[:, :, :, :, :, pl.ds(0, WIDTH)], GATHER_CUTS[0]),
            (value_ref, kv.at[:, :, :, :, :, pl.ds(WIDTH, WIDTH)], GATHER_CUTS[1]),
            (grad_b, every, GATHER_CUTS[2]),
        )
    )
    key_copy.wait()
    for part in key_parts:
        part.open()
    value_copy.wait()
    for part in value_parts:
        part.open()
    grad_copy.wait()
    grad_b[...] = grad_f[...].astype(BF16)
    for part in grad_parts:
        part.open()
    finish(small)
    gain = f32(gain_ref[...]).reshape(1, WIDTH)

    def norm_tile(i):
        hid_copy(i).wait()
        rows = pl.ds(pl.multiple_of(i * TILE, TILE), TILE)
        x = f32(hid[pl.ds(i * blocks, blocks)]).reshape(TILE, WIDTH)
        inv = lax.rsqrt(jnp.mean(x * x, axis=-1, keepdims=True) + 1e-06)
        inv_s[rows, :] = inv
        y = (x * inv) * gain
        nb[rows, :] = y.astype(BF16)
        nbt[:, rows] = y.T.astype(BF16)

    @pl.loop(0, tiles // 2)
    def _(i):
        norm_tile(i)

    for part in key_parts:
        part.ring(1)
    for part in value_parts:
        part.ring(1)

    @pl.loop(tiles // 2, tiles)
    def _(i):
        norm_tile(i)

    wq_copy = load(query_hbm, wq)
    for part in key_parts:
        part.ring(2)
    for part in value_parts:
        part.ring(2)
    for part in grad_parts:
        part.ring(1)

    row8 = lax.broadcasted_iota(jnp.int32, (SLOTS, WIDTH), 0)
    lane = lax.broadcasted_iota(jnp.int32, (SLOTS, WIDTH), 1)
    starts = jnp.zeros((SLOTS, WIDTH), jnp.int32)
    ends = jnp.zeros((SLOTS, WIDTH), jnp.int32)
    lane_last = jnp.full((SLOTS, HEAD_WIDTH), -1, jnp.int32)
    short_lane = lax.broadcasted_iota(jnp.int32, (SLOTS, HEAD_WIDTH), 1)
    hidden_last = jnp.zeros((SLOTS, WIDTH), F32)
    at = jnp.int32(0)
    for s in range(SLOTS):
        starts = jnp.where(row8 == s, at, starts)
        at = at + lengths[0, s]
        ends = jnp.where(row8 == s, at, ends)
        last = jnp.maximum(at - 1, 0)
        chosen = (short_lane % SLOTS == s) & (short_lane < 3 * SLOTS)
        lane_last = jnp.where(chosen, last, lane_last)
        block = f32(hid[last // SLOTS])
        picked = jnp.sum(jnp.where(row8 == last % SLOTS, block, 0.0), axis=0, keepdims=True)
        hidden_last = jnp.where(row8 == s, picked, hidden_last)
    member = (lane >= starts) & (lane < ends)
    inv_last = lax.rsqrt(jnp.mean(hidden_last * hidden_last, axis=-1, keepdims=True) + 1e-06)
    normed_last = hidden_last * inv_last
    last_b = (normed_last * gain).astype(BF16)

    finish(wq_copy)

    def spread(value, at, target):
        for part in range(value.shape[1] // HEAD_WIDTH):
            target[pl.ds(SLOTS * (at + part), SLOTS), :] = f32(
                value[:, part * HEAD_WIDTH : (part + 1) * HEAD_WIDTH].astype(BF16)
            )

    for n in range(4):
        spread(dot(last_b, wq[:, pl.ds(512 * n, 512)]), 4 * n, q_all)
    for part in key_parts:
        part.relay(2)
    for part in grad_parts:
        part.ring(2)
    for part in key_parts:
        part.close()
    for part in value_parts:
        part.relay(2)
    wo_copy = load(out_hbm, wo)
    for part in key_parts:
        finish(part.paired)

    def project(i, low):
        rows = pl.ds(pl.multiple_of(i * TILE, TILE), TILE)
        weight = kv[:, :, :, :, :, pl.ds(low, WIDTH)].reshape(WIDTH, WIDTH)
        joint[rows, pl.ds(low, WIDTH)] = dot(nb[rows, :], weight).astype(BF16)

    @pl.loop(0, tiles // 2)
    def _(i):
        project(i, 0)

    for part in value_parts:
        part.close()

    @pl.loop(tiles // 2, tiles)
    def _(i):
        project(i, 0)

    for part in value_parts:
        finish(part.paired)
    for part in grad_parts:
        part.relay(2)

    @pl.loop(0, tiles)
    def _(i):
        project(i, WIDTH)

    for part in grad_parts:
        part.close()

    def head(g, base=0):
        return pl.ds(base + g * HEAD_WIDTH, HEAD_WIDTH)

    def pair_rows(g):
        return pl.ds(2 * SLOTS * g, 2 * SLOTS)

    for g in range(KEY_HEADS):
        score[pair_rows(g), :] = dot(q_all[pair_rows(g), :].astype(BF16), joint[:, head(g)], 1, 1)
    scores = score[...].reshape(QUERY_HEADS, SLOTS, tokens) * scale_q
    scores = jnp.where(member[None], scores, -1e30)
    expo = jnp.exp(scores - jnp.max(scores, axis=-1, keepdims=True))
    probs = expo / jnp.sum(expo, axis=-1, keepdims=True)
    prob[...] = probs.reshape(QUERY_HEADS * SLOTS, tokens)

    def flatten(g, value):
        for q in range(2):
            flat[:, head(2 * g + q)] = value[q * SLOTS : (q + 1) * SLOTS, :]

    for g in range(KEY_HEADS):
        flatten(g, dot(prob[pair_rows(g), :].astype(BF16), joint[:, head(g, WIDTH)]))
    finish(wo_copy)
    pooled = hidden_last + dot(flat[...].astype(BF16), wo[...])
    for part in grad_parts:
        finish(part.paired)
    cached = jnp.zeros((SLOTS, WIDTH), F32)
    for s in range(SLOTS):
        o = owner[s]
        block = f32(every[o // 256, (o // 64) % RING, (o // 16) % RING, (o // 8) % 2])
        picked = jnp.sum(jnp.where(row8 == o % SLOTS, block, 0.0), axis=0, keepdims=True)
        cached = jnp.where(row8 == s, picked, cached)
    inv_len = lax.rsqrt(jnp.sum(pooled * pooled, axis=-1, keepdims=True) + 1e-06)
    embed = pooled * inv_len
    grad_pool = inv_len * (cached - embed * jnp.sum(embed * cached, axis=-1, keepdims=True))
    grad_pool_b = grad_pool.astype(BF16)
    for n in range(4):
        spread(dot(grad_pool_b, wo[pl.ds(512 * n, 512), :], 1, 1), 4 * n, a_all)

    def three(value):
        hi = f32(value.astype(BF16))
        mid = f32((value - hi).astype(BF16))
        rest = jnp.zeros((HEAD_WIDTH - 3 * SLOTS, WIDTH), F32)
        return jnp.concatenate([hi, mid, (value - hi) - mid, rest], axis=0).astype(BF16)

    pool_rows[...] = three(grad_pool)

    for g in range(KEY_HEADS):
        score[pair_rows(g), :] = dot(
            a_all[pair_rows(g), :].astype(BF16), joint[:, head(g, WIDTH)], 1, 1
        )
        both[:, head(g, WIDTH)] = dot(
            prob[pair_rows(g), :].astype(BF16), a_all[pair_rows(g), :].astype(BF16), 0, 0
        ).astype(BF16)
    grad_prob = score[...]
    probs = prob[...]
    inner = jnp.sum(probs * grad_prob, axis=-1, keepdims=True)
    gscore[...] = (probs * (grad_prob - inner) * scale_q).astype(BF16)
    for g in range(KEY_HEADS):
        both[:, head(g)] = dot(
            gscore[pair_rows(g), :], q_all[pair_rows(g), :].astype(BF16), 0, 0
        ).astype(BF16)

    def share_part(part):
        low, size = SCATTER_CUTS[part]

        @pl.loop(0, RING)
        def _(x):
            rows = pl.ds(pl.multiple_of(x * TILE, TILE), TILE)
            value = dot(nbt[rows, :], both[:, pl.ds(low, size)])
            share[x, :, :, :, :, pl.ds(low, size)] = value.reshape(
                RING, RING, 2, SLOTS, size
            ).astype(BF16)
            weight = f32(kv[x, :, :, :, :, pl.ds(low, size)]).reshape(TILE, size)
            product = value * weight
            total = product[:, :HEAD_WIDTH]
            for n in range(1, size // HEAD_WIDTH):
                total = total + product[:, n * HEAD_WIDTH : (n + 1) * HEAD_WIDTH]
            if part == 0:
                gain_acc[rows, :] = total
            else:
                gain_acc[rows, :] += total

        return net.send(
            share.at[:, :, :, 1 - net.core, :, pl.ds(low, size)], pair_in[part], net.sibling
        )

    flights = [[], [], []]
    early = [[], [], []]

    def halves(part):
        pairs[part].wait()
        low, size = SCATTER_CUTS[part]
        order = ORDERS[part]

        @pl.loop(0, RING * RING)
        def _(at):
            ahead = [at // RING, at % RING, 0]
            for z in range(RING):
                ahead[2] = z
                value = f32(share[ahead[0], ahead[1], z, net.core, :, pl.ds(low, size)])
                value = value + f32(pair_in[part][ahead[0], ahead[1], z])
                first[part][ahead[order[0]], ahead[order[1]], ahead[order[2]]] = value.astype(BF16)

        dim = order[0]
        for half, delta in ((0, 1), (1, 3)):
            flights[part].append(
                net.send(
                    first[part].at[net.at(dim, 2), pl.ds(2 * half, 2)],
                    relay_in[part].at[half],
                    net.peer(dim, delta),
                )
            )
            early[part].append(
                net.send(
                    first[part].at[net.at(dim, delta), pl.ds(2 - 2 * half, 2)],
                    first_in[part].at[half, pl.ds(2 - 2 * half, 2)],
                    net.peer(dim, delta),
                )
            )

    def passed(part):
        finish(flights[part])
        dim = ORDERS[part][0]
        for half, delta in ((0, 1), (1, 3)):
            there = net.at(dim, delta)
            for a in range(2):
                row = 2 * half + a
                value = f32(first[part][there, row]) + f32(relay_in[part][half, a])
                first[part][there, row] = value.astype(BF16)
            flights[part].append(
                net.send(
                    first[part].at[there, pl.ds(2 * half, 2)],
                    first_in[part].at[half, pl.ds(2 * half, 2)],
                    net.peer(dim, delta),
                )
            )

    def push(part, step, source, target):
        dim = ORDERS[part][step]
        for delta in (2, 1, 3):
            flights[part].append(
                net.send(source.at[net.at(dim, delta)], target.at[delta - 1], net.peer(dim, delta))
            )

    def summed(part):
        finish(flights[part])
        finish(early[part])
        mine = net.coords[ORDERS[part][0]]
        for a in range(RING):
            value = f32(first[part][mine, a])
            value = value + (f32(first_in[part][0, a]) + f32(first_in[part][1, a]))
            second[part][a] = value.astype(BF16)
        push(part, 1, second[part], second_in[part])

    def summed_again(part):
        finish(flights[part])
        mine = net.coords[ORDERS[part][1]]
        value = f32(second[part][mine]) + f32(second_in[part][0])
        value = value + (f32(second_in[part][1]) + f32(second_in[part][2]))
        third[part][...] = value.astype(BF16)
        push(part, 2, third[part], third_in[part])

    def summed_last(part):
        low, size = SCATTER_CUTS[part]
        finish(flights[part])
        mine = net.coords[ORDERS[part][2]]
        value = f32(third[part][mine]) + f32(third_in[part][0])
        value = value + (f32(third_in[part][1]) + f32(third_in[part][2]))
        packed[:SLOTS, pl.ds(low, size)] = value

    def gain_round(dim, value):
        gain_sum[dim + 1] = value
        gain_in[dim, net.coords[dim]] = value
        return [
            net.send(
                gain_sum.at[dim + 1], gain_in.at[dim, net.coords[dim]], net.peer(dim, delta)
            )
            for delta in range(1, RING)
        ]

    def gain_total(dim, copies):
        finish(copies)
        return (gain_in[dim, 0] + gain_in[dim, 1]) + (gain_in[dim, 2] + gain_in[dim, 3])

    out_copies = []

    def input_grad(i):
        rows = pl.ds(i * TILE, TILE)
        weight = kv[...].reshape(WIDTH, 2 * WIDTH)
        tall = lax.broadcasted_iota(jnp.int32, (TILE, HEAD_WIDTH), 0) + i * TILE
        hot = jnp.where(tall == lane_last[:1], 1.0, 0.0).astype(BF16)
        grad_normed = dot(both[rows, :], weight, 1, 1) + dot(hot, select_rows[...])
        inv = inv_s[rows, :]
        normed = f32(hid[pl.ds(i * blocks, blocks)]).reshape(TILE, WIDTH) * inv
        scaled = grad_normed * gain
        mean = jnp.mean(scaled * normed, axis=-1, keepdims=True)
        value = inv * (scaled - normed * mean) + dot(hot, pool_rows[...])
        result[rows, :] = value.astype(BF16)
        out_copies.append(net.local(result.at[rows], grad_in.at[rows]))

    pairs = [share_part(0), share_part(1)]
    halves(0)
    pairs.append(share_part(2))
    halves(1)
    for g in range(KEY_HEADS):
        flatten(g, dot(gscore[pair_rows(g), :], joint[:, head(g)]))
    query_back = dot(flat[...].astype(BF16), wq[...], 1, 1)
    select_rows[...] = three(query_back)
    gain_part = jnp.sum(gain_acc[...].T, axis=0, keepdims=True) / gain
    gain_part = gain_part + jnp.sum(query_back * normed_last, axis=0, keepdims=True)
    gain_sum[0] = gain_part
    gain_copies = [net.send(gain_sum.at[0], gain_pair, net.sibling)]
    halves(2)
    passed(0)
    input_grad(0)
    finish(gain_copies)
    gain_copies = gain_round(0, gain_sum[0] + gain_pair[...])
    passed(1)
    passed(2)
    summed(0)
    input_grad(1)
    gain_copies = gain_round(1, gain_total(0, gain_copies))
    summed(1)
    summed(2)
    summed_again(0)
    input_grad(2)
    gain_copies = gain_round(2, gain_total(1, gain_copies))
    summed_again(1)
    summed_again(2)
    input_grad(3)
    packed[SLOTS : SLOTS + 1, :WIDTH] = gain_total(2, gain_copies)
    for part in range(3):
        summed_last(part)
    finish(out_copies)


def per_device(
    hidden_in, lengths, owner, pooled_grad, norm_gain, w_query, w_key, value_weight, w_out
):
    tokens, width = hidden_in.shape
    heads = QUERY_HEADS * SLOTS
    grid = (RING, RING, RING, 2, SLOTS)

    def vmem(*shape, kind=BF16):
        return pltpu.VMEM(shape, kind)

    def parts(*lead):
        return [vmem(*lead, SLOTS, size) for _, size in SCATTER_CUTS]

    spec = pl.BlockSpec(memory_space=pltpu.VMEM)
    hbm = pl.BlockSpec(memory_space=pltpu.HBM)
    whole = pl.BlockSpec(memory_space=pl.ANY)
    grad_in, packed = pl.pallas_call(
        step_kernel,
        out_shape=(
            jax.ShapeDtypeStruct((tokens, width), BF16),
            jax.ShapeDtypeStruct((2 * SLOTS, 2 * WIDTH), F32),
        ),
        in_specs=[hbm] * 9,
        out_specs=(whole, spec),
        scratch_shapes=[
            vmem(tokens // SLOTS, SLOTS, width),
            vmem(width, 2 * WIDTH),
            vmem(2 * WIDTH, width),
            vmem(*grid, 2 * WIDTH),
            vmem(*grid, width),
            vmem(SLOTS, width),
            vmem(tokens, width),
            vmem(width, tokens),
            vmem(tokens, 1, kind=F32),
            vmem(tokens, 2 * WIDTH),
            vmem(tokens, 2 * WIDTH),
            vmem(tokens, width),
            vmem(heads, tokens, kind=F32),
            vmem(heads, tokens, kind=F32),
            vmem(heads, tokens),
            vmem(heads, HEAD_WIDTH, kind=F32),
            vmem(heads, HEAD_WIDTH, kind=F32),
            vmem(SLOTS, 2 * WIDTH, kind=F32),
            vmem(SLOTS, 2 * WIDTH),
            vmem(HEAD_WIDTH, width),
            vmem(HEAD_WIDTH, width),
            vmem(*grid, 2 * WIDTH),
            vmem(width, HEAD_WIDTH, kind=F32),
            vmem(1, width, kind=F32),
            vmem(4, 1, width, kind=F32),
            vmem(3, RING, 1, width, kind=F32),
            pltpu.SemaphoreType.DMA((2, 256)),
        ]
        + parts(RING, RING, RING)
        + parts(RING, RING, RING)
        + parts(2, 2, RING)
        + parts(2, RING, RING)
        + parts(RING, RING)
        + parts(RING - 1, RING)
        + parts(RING)
        + parts(RING - 1)
        + [
            pltpu.SMEM((1, SLOTS), jnp.int32),
            pltpu.SMEM((SLOTS,), jnp.int32),
            vmem(SLOTS, width, kind=F32),
            vmem(width),
            vmem(SLOTS, WIDTH),
            vmem(SLOTS, WIDTH),
            pltpu.SemaphoreType.DMA((tokens // TILE,)),
        ],
        compiler_params=pltpu.CompilerParams(
            collective_id=0, has_side_effects=True, vmem_limit_bytes=50 * 2**20
        ),
        name="step",
    )(
        *(
            pltpu.with_memory_space_constraint(value, pltpu.HBM)
            for value in (
                lengths,
                owner,
                hidden_in.reshape(tokens // SLOTS, SLOTS, width),
                pooled_grad,
                norm_gain,
                w_query,
                w_key,
                value_weight,
                w_out,
            )
        )
    )
    return grad_in, packed[:SLOTS, :WIDTH], packed[:SLOTS, WIDTH:], packed[SLOTS, :WIDTH]


def solution(mesh):
    return jax.shard_map(
        per_device,
        mesh=mesh,
        in_specs=(
            P("dp", None),
            P("dp", None),
            P("dp"),
            P("dp", None),
            P(),
            P(),
            P("dp", None),
            P("dp", None),
            P(),
        ),
        out_specs=(P("dp", None), P("dp", None), P("dp", None), P()),
        check_vma=False,
    )
```

```python
import functools
import jax
import jax.numpy as jnp
from jax import lax
from jax.experimental import pallas as pl
from jax.experimental.pallas import tpu as pltpu
from jax.sharding import PartitionSpec as P

QUERY_HEADS = 16
KEY_HEADS = 8
HEAD_WIDTH = 128
WIDTH = KEY_HEADS * HEAD_WIDTH
SLOTS = 8
TILE = 256
RING = 4
STRIDES = (32, 8, 2)
ORDERS = ((0, 1, 2), (1, 2, 0), (2, 0, 1))
MESH = pl.DeviceIdType.MESH
BF16, F32 = jnp.bfloat16, jnp.float32
WEIGHT_CUTS = ((0, 768), (768, 640), (1408, 640))
GRAD_CUTS = ((0, 256), (256, 384), (640, 384))
SCATTER_CUTS = ((0, 768), (768, 768), (1536, 512))


def f32(value):
    return value.astype(F32)


def dot(a, b, ca=1, cb=0):
    return lax.dot_general(a, b, (((ca,), (cb,)), ((), ())), preferred_element_type=F32)


class Net:
    def __init__(self, sems):
        self.sems, self.used = sems, 0
        me = lax.axis_index("dp")
        self.me = me
        self.coords = ((me // 32) % RING, (me // 8) % RING, (me // 2) % RING)
        self.core = me % 2
        self.sibling = me + 1 - 2 * self.core

    def at(self, dim, delta):
        return (self.coords[dim] + delta + RING) % RING

    def peer(self, dim, delta):
        return self.me + (self.at(dim, delta) - self.coords[dim]) * STRIDES[dim]

    def greet(self):
        barrier = pltpu.get_barrier_semaphore()
        pl.semaphore_signal(barrier, inc=1, device_id=(self.sibling,), device_id_type=MESH)
        for dim in range(3):
            for delta in range(1, RING):
                pl.semaphore_signal(
                    barrier, inc=1, device_id=(self.peer(dim, delta),), device_id_type=MESH
                )
        pl.semaphore_wait(barrier, 10)

    def send(self, src, dst, other):
        copy = pltpu.make_async_remote_copy(
            src_ref=src,
            dst_ref=dst,
            send_sem=self.sems.at[0, self.used],
            recv_sem=self.sems.at[1, self.used],
            device_id=(other,),
            device_id_type=MESH,
        )
        self.used += 1
        copy.start()
        return copy

    def local(self, src, dst):
        copy = pltpu.make_async_copy(src, dst, self.sems.at[0, self.used])
        self.used += 1
        copy.start()
        return copy


def finish(copies):
    for copy in copies:
        copy.wait()
    copies.clear()


class Gather:
    def __init__(self, net, source, target, low, size, order):
        self.net, self.order = net, order
        self.source = source.at[:, pl.ds(low, size)]
        self.target = target.at[:, :, :, :, :, pl.ds(low, size)]
        self.flying, self.paired = [], []

    def slab(self, done, dim=None, delta=0, half=None):
        net = self.net
        index = [net.coords[0], net.coords[1], net.coords[2], net.core]
        if dim is not None:
            index[dim] = net.at(dim, delta)
        for at in done:
            index[at] = slice(None)
        if half is not None:
            index[done[0]] = pl.ds(half * 2, 2)
        return self.target.at[tuple(index)]

    def open(self):
        net, mine = self.net, self.slab(())
        self.own = net.local(self.source, mine)
        for delta in (2, 1, 3):
            self.flying.append(net.send(self.source, mine, net.peer(self.order[0], delta)))

    def pair(self, step, delta):
        piece = self.slab(self.order[:step], self.order[step], delta)
        self.paired.append(self.net.send(piece, piece, self.net.sibling))

    def ring(self, step):
        if step == 1:
            self.own.wait()
        finish(self.flying)
        dim, piece = self.order[step], self.slab(self.order[:step])
        for delta in (2, 1, 3):
            self.flying.append(self.net.send(piece, piece, self.net.peer(dim, delta)))
        if step == 2:
            self.pair(2, 0)

    def relay(self, step):
        if step == 2:
            self.flying[1].wait()
            self.pair(2, 3)
            self.flying[2].wait()
            self.pair(2, 1)

    def close(self):
        self.flying[0].wait()
        self.pair(2, 2)


def step_kernel(
    lengths_hbm,
    owner_hbm,
    hidden_hbm,
    grad_hbm,
    gain_hbm,
    query_hbm,
    key_hbm,
    value_hbm,
    out_hbm,
    grad_in,
    packed,
    *scratch,
):
    (hid, wq, wo, kv, every, grad_b, nb, nbt, inv_s, joint, both, result) = scratch[:12]
    (score, prob, gscore, q_all, a_all, flat, flat_b, select_rows, pool_rows) = scratch[12:21]
    (share, gain_acc, gain_pair, gain_sum, gain_in, sems) = scratch[21:27]
    pair_in, first, relay_in, first_in, second, second_in, third, third_in = (
        scratch[27 + 3 * i : 30 + 3 * i] for i in range(8)
    )
    lengths, owner, grad_f, gain_ref, weight_ref, hid_sems = scratch[51:]
    net = Net(sems)
    scale_q = 1.0 / HEAD_WIDTH**0.5
    tokens = nb.shape[0]
    tiles = tokens // TILE
    blocks = TILE // SLOTS

    weight_copies = [
        net.local(key_hbm, weight_ref.at[:, pl.ds(0, WIDTH)]),
        net.local(value_hbm, weight_ref.at[:, pl.ds(WIDTH, WIDTH)]),
    ]
    grad_copy = net.local(grad_hbm, grad_f)
    small = [
        net.local(gain_hbm, gain_ref),
        net.local(lengths_hbm, lengths),
        net.local(owner_hbm, owner),
    ]

    def hid_copy(i):
        part = pl.ds(i * blocks, blocks)
        return pltpu.make_async_copy(hidden_hbm.at[part], hid.at[part], hid_sems.at[i])

    for i in range(tiles):
        hid_copy(i).start()

    def load(src, dst):
        rows = dst.shape[0] // 4
        return [
            net.local(src.at[pl.ds(n * rows, rows)], dst.at[pl.ds(n * rows, rows)])
            for n in range(4)
        ]

    net.greet()
    weight_parts, grad_parts = (
        [
            Gather(net, source, target, low, size, ORDERS[part])
            for part, (low, size) in enumerate(cuts)
        ]
        for source, target, cuts in (
            (weight_ref, kv, WEIGHT_CUTS),
            (grad_b, every, GRAD_CUTS),
        )
    )
    finish(weight_copies)
    for part in weight_parts:
        part.open()
    grad_copy.wait()
    grad_b[...] = grad_f[...].astype(BF16)
    for part in grad_parts:
        part.open()
    finish(small)
    gain = f32(gain_ref[...]).reshape(1, WIDTH)

    def norm_tile(i):
        hid_copy(i).wait()
        rows = pl.ds(pl.multiple_of(i * TILE, TILE), TILE)
        x = f32(hid[pl.ds(i * blocks, blocks)]).reshape(TILE, WIDTH)
        inv = lax.rsqrt(jnp.mean(x * x, axis=-1, keepdims=True) + 1e-06)
        inv_s[rows, :] = inv
        y = (x * inv) * gain
        nb[rows, :] = y.astype(BF16)
        nbt[:, rows] = y.T.astype(BF16)

    @pl.loop(0, tiles // 2)
    def _(i):
        norm_tile(i)

    for part in weight_parts:
        part.ring(1)

    @pl.loop(tiles // 2, tiles)
    def _(i):
        norm_tile(i)

    wq_copy = load(query_hbm, wq)
    for part in weight_parts:
        part.ring(2)
    for part in grad_parts:
        part.ring(1)

    row8 = lax.broadcasted_iota(jnp.int32, (SLOTS, WIDTH), 0)
    lane = lax.broadcasted_iota(jnp.int32, (SLOTS, WIDTH), 1)
    starts = jnp.zeros((SLOTS, WIDTH), jnp.int32)
    ends = jnp.zeros((SLOTS, WIDTH), jnp.int32)
    lane_last = jnp.full((SLOTS, HEAD_WIDTH), -1, jnp.int32)
    short_lane = lax.broadcasted_iota(jnp.int32, (SLOTS, HEAD_WIDTH), 1)
    hidden_last = jnp.zeros((SLOTS, WIDTH), F32)
    at = jnp.int32(0)
    for s in range(SLOTS):
        starts = jnp.where(row8 == s, at, starts)
        at = at + lengths[0, s]
        ends = jnp.where(row8 == s, at, ends)
        last = jnp.maximum(at - 1, 0)
        chosen = (short_lane % SLOTS == s) & (short_lane < 3 * SLOTS)
        lane_last = jnp.where(chosen, last, lane_last)
        block = f32(hid[last // SLOTS])
        picked = jnp.sum(jnp.where(row8 == last % SLOTS, block, 0.0), axis=0, keepdims=True)
        hidden_last = jnp.where(row8 == s, picked, hidden_last)
    member = (lane >= starts) & (lane < ends)
    inv_last = lax.rsqrt(jnp.mean(hidden_last * hidden_last, axis=-1, keepdims=True) + 1e-06)
    normed_last = hidden_last * inv_last
    last_b = (normed_last * gain).astype(BF16)

    finish(wq_copy)

    def spread(value, at, target):
        for part in range(value.shape[1] // HEAD_WIDTH):
            target[pl.ds(SLOTS * (at + part), SLOTS), :] = f32(
                value[:, part * HEAD_WIDTH : (part + 1) * HEAD_WIDTH].astype(BF16)
            )

    for n in range(4):
        spread(dot(last_b, wq[:, pl.ds(512 * n, 512)]), 4 * n, q_all)
    for part in weight_parts:
        part.relay(2)
    for part in grad_parts:
        part.ring(2)
    for part in weight_parts:
        part.close()
    wo_copy = load(out_hbm, wo)
    for part in weight_parts:
        finish(part.paired)

    def project(i, low):
        rows = pl.ds(pl.multiple_of(i * TILE, TILE), TILE)
        weight = kv[:, :, :, :, :, pl.ds(low, WIDTH)].reshape(WIDTH, WIDTH)
        joint[rows, pl.ds(low, WIDTH)] = dot(nb[rows, :], weight).astype(BF16)

    @pl.loop(0, tiles)
    def _(i):
        project(i, 0)

    for part in grad_parts:
        part.relay(2)

    @pl.loop(0, tiles)
    def _(i):
        project(i, WIDTH)

    for part in grad_parts:
        part.close()

    def head(g, base=0):
        return pl.ds(base + g * HEAD_WIDTH, HEAD_WIDTH)

    def pair_rows(g):
        return pl.ds(2 * SLOTS * g, 2 * SLOTS)

    for g in range(KEY_HEADS):
        score[pair_rows(g), :] = dot(q_all[pair_rows(g), :].astype(BF16), joint[:, head(g)], 1, 1)
    scores = score[...].reshape(QUERY_HEADS, SLOTS, tokens) * scale_q
    scores = jnp.where(member[None], scores, -1e30)
    expo = jnp.exp(scores - jnp.max(scores, axis=-1, keepdims=True))
    probs = expo / jnp.sum(expo, axis=-1, keepdims=True)
    prob[...] = probs.reshape(QUERY_HEADS * SLOTS, tokens)

    def flatten(g, value):
        for q in range(2):
            flat[:, head(2 * g + q)] = value[q * SLOTS : (q + 1) * SLOTS, :]

    for g in range(KEY_HEADS):
        flatten(g, dot(prob[pair_rows(g), :].astype(BF16), joint[:, head(g, WIDTH)]))
    finish(wo_copy)
    pooled = hidden_last + dot(flat[...].astype(BF16), wo[...])
    for part in grad_parts:
        finish(part.paired)
    cached = jnp.zeros((SLOTS, WIDTH), F32)
    for s in range(SLOTS):
        o = owner[s]
        block = f32(every[o // 256, (o // 64) % RING, (o // 16) % RING, (o // 8) % 2])
        picked = jnp.sum(jnp.where(row8 == o % SLOTS, block, 0.0), axis=0, keepdims=True)
        cached = jnp.where(row8 == s, picked, cached)
    inv_len = lax.rsqrt(jnp.sum(pooled * pooled, axis=-1, keepdims=True) + 1e-06)
    embed = pooled * inv_len
    grad_pool = inv_len * (cached - embed * jnp.sum(embed * cached, axis=-1, keepdims=True))
    grad_pool_b = grad_pool.astype(BF16)
    for n in range(4):
        spread(dot(grad_pool_b, wo[pl.ds(512 * n, 512), :], 1, 1), 4 * n, a_all)

    def three(value):
        hi = f32(value.astype(BF16))
        mid = f32((value - hi).astype(BF16))
        rest = jnp.zeros((HEAD_WIDTH - 3 * SLOTS, WIDTH), F32)
        return jnp.concatenate([hi, mid, (value - hi) - mid, rest], axis=0).astype(BF16)

    pool_rows[...] = three(grad_pool)

    for g in range(KEY_HEADS):
        score[pair_rows(g), :] = dot(
            a_all[pair_rows(g), :].astype(BF16), joint[:, head(g, WIDTH)], 1, 1
        )
        both[:, head(g, WIDTH)] = dot(
            prob[pair_rows(g), :].astype(BF16), a_all[pair_rows(g), :].astype(BF16), 0, 0
        ).astype(BF16)
    grad_prob = score[...]
    probs = prob[...]
    inner = jnp.sum(probs * grad_prob, axis=-1, keepdims=True)
    gscore[...] = (probs * (grad_prob - inner) * scale_q).astype(BF16)
    for g in range(KEY_HEADS):
        both[:, head(g)] = dot(
            gscore[pair_rows(g), :], q_all[pair_rows(g), :].astype(BF16), 0, 0
        ).astype(BF16)

    def share_part(part):
        low, size = SCATTER_CUTS[part]

        @pl.loop(0, RING)
        def _(x):
            rows = pl.ds(pl.multiple_of(x * TILE, TILE), TILE)
            value = dot(nbt[rows, :], both[:, pl.ds(low, size)])
            share[x, :, :, :, :, pl.ds(low, size)] = value.reshape(
                RING, RING, 2, SLOTS, size
            ).astype(BF16)
            weight = f32(kv[x, :, :, :, :, pl.ds(low, size)]).reshape(TILE, size)
            product = value * weight
            total = product[:, :HEAD_WIDTH]
            for n in range(1, size // HEAD_WIDTH):
                total = total + product[:, n * HEAD_WIDTH : (n + 1) * HEAD_WIDTH]
            if part == 0:
                gain_acc[rows, :] = total
            else:
                gain_acc[rows, :] += total

        return net.send(
            share.at[:, :, :, 1 - net.core, :, pl.ds(low, size)], pair_in[part], net.sibling
        )

    flights = [[], [], []]
    early = [[], [], []]

    def halves(part):
        pairs[part].wait()
        low, size = SCATTER_CUTS[part]
        order = ORDERS[part]

        @pl.loop(0, RING * RING)
        def _(at):
            ahead = [at // RING, at % RING, 0]
            for z in range(RING):
                ahead[2] = z
                value = f32(share[ahead[0], ahead[1], z, net.core, :, pl.ds(low, size)])
                value = value + f32(pair_in[part][ahead[0], ahead[1], z])
                first[part][ahead[order[0]], ahead[order[1]], ahead[order[2]]] = value.astype(BF16)

        dim = order[0]
        for half, delta in ((0, 1), (1, 3)):
            flights[part].append(
                net.send(
                    first[part].at[net.at(dim, 2), pl.ds(2 * half, 2)],
                    relay_in[part].at[half],
                    net.peer(dim, delta),
                )
            )
            early[part].append(
                net.send(
                    first[part].at[net.at(dim, delta), pl.ds(2 - 2 * half, 2)],
                    first_in[part].at[half, pl.ds(2 - 2 * half, 2)],
                    net.peer(dim, delta),
                )
            )

    def passed(part):
        finish(flights[part])
        dim = ORDERS[part][0]
        for half, delta in ((0, 1), (1, 3)):
            there = net.at(dim, delta)
            for a in range(2):
                row = 2 * half + a
                value = f32(first[part][there, row]) + f32(relay_in[part][half, a])
                first[part][there, row] = value.astype(BF16)
            flights[part].append(
                net.send(
                    first[part].at[there, pl.ds(2 * half, 2)],
                    first_in[part].at[half, pl.ds(2 * half, 2)],
                    net.peer(dim, delta),
                )
            )

    def push(part, step, source, target):
        dim = ORDERS[part][step]
        for delta in (2, 1, 3):
            flights[part].append(
                net.send(source.at[net.at(dim, delta)], target.at[delta - 1], net.peer(dim, delta))
            )

    def summed(part):
        finish(flights[part])
        finish(early[part])
        mine = net.coords[ORDERS[part][0]]
        for a in range(RING):
            value = f32(first[part][mine, a])
            value = value + (f32(first_in[part][0, a]) + f32(first_in[part][1, a]))
            second[part][a] = value.astype(BF16)
        push(part, 1, second[part], second_in[part])

    def summed_again(part):
        finish(flights[part])
        mine = net.coords[ORDERS[part][1]]
        value = f32(second[part][mine]) + f32(second_in[part][0])
        value = value + (f32(second_in[part][1]) + f32(second_in[part][2]))
        third[part][...] = value.astype(BF16)
        push(part, 2, third[part], third_in[part])

    def summed_last(part):
        low, size = SCATTER_CUTS[part]
        finish(flights[part])
        mine = net.coords[ORDERS[part][2]]
        value = f32(third[part][mine]) + f32(third_in[part][0])
        value = value + (f32(third_in[part][1]) + f32(third_in[part][2]))
        packed[:SLOTS, pl.ds(low, size)] = value

    def gain_round(dim, value):
        gain_sum[dim + 1] = value
        gain_in[dim, net.coords[dim]] = value
        return [
            net.send(
                gain_sum.at[dim + 1], gain_in.at[dim, net.coords[dim]], net.peer(dim, delta)
            )
            for delta in range(1, RING)
        ]

    def gain_total(dim, copies):
        finish(copies)
        return (gain_in[dim, 0] + gain_in[dim, 1]) + (gain_in[dim, 2] + gain_in[dim, 3])

    out_copies = []

    def input_grad(i):
        rows = pl.ds(i * TILE, TILE)
        weight = kv[...].reshape(WIDTH, 2 * WIDTH)
        tall = lax.broadcasted_iota(jnp.int32, (TILE, HEAD_WIDTH), 0) + i * TILE
        hot = jnp.where(tall == lane_last[:1], 1.0, 0.0).astype(BF16)
        grad_normed = dot(both[rows, :], weight, 1, 1) + dot(hot, select_rows[...])
        inv = inv_s[rows, :]
        normed = f32(hid[pl.ds(i * blocks, blocks)]).reshape(TILE, WIDTH) * inv
        scaled = grad_normed * gain
        mean = jnp.mean(scaled * normed, axis=-1, keepdims=True)
        value = inv * (scaled - normed * mean) + dot(hot, pool_rows[...])
        result[rows, :] = value.astype(BF16)
        out_copies.append(net.local(result.at[rows], grad_in.at[rows]))

    pairs = [share_part(0), share_part(1)]
    halves(0)
    pairs.append(share_part(2))
    halves(1)
    for g in range(KEY_HEADS):
        flatten(g, dot(gscore[pair_rows(g), :], joint[:, head(g)]))
    query_back = dot(flat[...].astype(BF16), wq[...], 1, 1)
    select_rows[...] = three(query_back)
    gain_part = jnp.sum(gain_acc[...].T, axis=0, keepdims=True) / gain
    gain_part = gain_part + jnp.sum(query_back * normed_last, axis=0, keepdims=True)
    gain_sum[0] = gain_part
    gain_copies = [net.send(gain_sum.at[0], gain_pair, net.sibling)]
    halves(2)
    input_grad(0)
    passed(0)
    passed(1)
    finish(gain_copies)
    gain_copies = gain_round(0, gain_sum[0] + gain_pair[...])
    passed(2)
    input_grad(1)
    gain_copies = gain_round(1, gain_total(0, gain_copies))
    summed(0)
    summed(1)
    summed(2)
    input_grad(2)
    gain_copies = gain_round(2, gain_total(1, gain_copies))
    summed_again(0)
    summed_again(1)
    summed_again(2)
    input_grad(3)
    packed[SLOTS : SLOTS + 1, :WIDTH] = gain_total(2, gain_copies)
    for part in range(3):
        summed_last(part)
    finish(out_copies)


def per_device(
    hidden_in, lengths, owner, pooled_grad, norm_gain, w_query, w_key, value_weight, w_out
):
    tokens, width = hidden_in.shape
    heads = QUERY_HEADS * SLOTS
    grid = (RING, RING, RING, 2, SLOTS)

    def vmem(*shape, kind=BF16):
        return pltpu.VMEM(shape, kind)

    def parts(*lead):
        return [vmem(*lead, SLOTS, size) for _, size in SCATTER_CUTS]

    spec = pl.BlockSpec(memory_space=pltpu.VMEM)
    hbm = pl.BlockSpec(memory_space=pltpu.HBM)
    whole = pl.BlockSpec(memory_space=pl.ANY)
    grad_in, packed = pl.pallas_call(
        step_kernel,
        out_shape=(
            jax.ShapeDtypeStruct((tokens, width), BF16),
            jax.ShapeDtypeStruct((2 * SLOTS, 2 * WIDTH), F32),
        ),
        in_specs=[hbm] * 9,
        out_specs=(whole, spec),
        scratch_shapes=[
            vmem(tokens // SLOTS, SLOTS, width),
            vmem(width, 2 * WIDTH),
            vmem(2 * WIDTH, width),
            vmem(*grid, 2 * WIDTH),
            vmem(*grid, width),
            vmem(SLOTS, width),
            vmem(tokens, width),
            vmem(width, tokens),
            vmem(tokens, 1, kind=F32),
            vmem(tokens, 2 * WIDTH),
            vmem(tokens, 2 * WIDTH),
            vmem(tokens, width),
            vmem(heads, tokens, kind=F32),
            vmem(heads, tokens, kind=F32),
            vmem(heads, tokens),
            vmem(heads, HEAD_WIDTH, kind=F32),
            vmem(heads, HEAD_WIDTH, kind=F32),
            vmem(SLOTS, 2 * WIDTH, kind=F32),
            vmem(SLOTS, 2 * WIDTH),
            vmem(HEAD_WIDTH, width),
            vmem(HEAD_WIDTH, width),
            vmem(*grid, 2 * WIDTH),
            vmem(width, HEAD_WIDTH, kind=F32),
            vmem(1, width, kind=F32),
            vmem(4, 1, width, kind=F32),
            vmem(3, RING, 1, width, kind=F32),
            pltpu.SemaphoreType.DMA((2, 256)),
        ]
        + parts(RING, RING, RING)
        + parts(RING, RING, RING)
        + parts(2, 2, RING)
        + parts(2, RING, RING)
        + parts(RING, RING)
        + parts(RING - 1, RING)
        + parts(RING)
        + parts(RING - 1)
        + [
            pltpu.SMEM((1, SLOTS), jnp.int32),
            pltpu.SMEM((SLOTS,), jnp.int32),
            vmem(SLOTS, width, kind=F32),
            vmem(width),
            vmem(SLOTS, 2 * WIDTH),
            pltpu.SemaphoreType.DMA((tokens // TILE,)),
        ],
        compiler_params=pltpu.CompilerParams(
            collective_id=0, has_side_effects=True, vmem_limit_bytes=50 * 2**20
        ),
        name="step",
    )(
        *(
            pltpu.with_memory_space_constraint(value, pltpu.HBM)
            for value in (
                lengths,
                owner,
                hidden_in.reshape(tokens // SLOTS, SLOTS, width),
                pooled_grad,
                norm_gain,
                w_query,
                w_key,
                value_weight,
                w_out,
            )
        )
    )
    return grad_in, packed[:SLOTS, :WIDTH], packed[:SLOTS, WIDTH:], packed[SLOTS, :WIDTH]


def solution(mesh):
    return jax.shard_map(
        per_device,
        mesh=mesh,
        in_specs=(
            P("dp", None),
            P("dp", None),
            P("dp"),
            P("dp", None),
            P(),
            P(),
            P("dp", None),
            P("dp", None),
            P(),
        ),
        out_specs=(P("dp", None), P("dp", None), P("dp", None), P()),
        check_vma=False,
    )
```
